32 devices in a mesh: parts: 2 (over y), expert: 4 (over z), hidden: 2 (over x), rep: 2 (over core).
Axes of the slice: x: 2, y: 2, z: 4, core: 2. Of those that a mesh axis runs over, the one named last changes fastest.
Arguments:
- tokens: bfloat16 [1024, 4096], P(('parts', 'expert', 'rep'), 'hidden'), parts along dimension 0, may hold values from -6 to 6
- route_ids: int32 [1024, 2], P(('parts', 'expert', 'rep')), parts along dimension 0, may hold values from 0 to 3, all different within a row; in each aligned block of 64 rows (0 to 63, 64 to 127, ...) at most 48 rows name the same one
- route_weight: float32 [1024, 2], P(('parts', 'expert', 'rep')), parts along dimension 0, may hold values from 0.1 to 1
- user_slot: int32 [128, 4], P(('parts', 'expert', 'rep')), parts along dimension 0, may hold values from 0 to 15
- gate_weight: bfloat16 [4, 4096, 1536], P('expert', None, 'hidden'), may hold values from -0.09375 to 0.09375
- up_weight: bfloat16 [4, 4096, 1536], P('expert', None, 'hidden'), may hold values from -0.09375 to 0.09375
- down_weight: bfloat16 [4, 1536, 4096], P('expert', 'hidden'), may hold values from -0.15625 to 0.15625
- adapter_down: bfloat16 [4, 4096, 128], P('expert', 'hidden'), may hold values from -0.09375 to 0.09375
- adapter_up: bfloat16 [4, 128, 1536], P('expert', None, 'hidden'), may hold values from -2 to 2
Outputs:
- mixed: bfloat16 [1024, 4096], P(('parts', 'expert', 'rep'), 'hidden'), parts along dimension 0
The draws below stay inside these ranges and needn't reach their ends.
There are 2 independent parts, one for each index of `parts`. The reference program is written for one: setup_inputs(seed, part) draws one part's arguments, and reference() takes and returns one part's arrays. A program takes and returns all parts, laid end to end along the dimension named above; an argument that names none is the same for every part. Nothing has to cross between parts.
Inputs may be any that keep to these rules, and one draw needn't show every extreme that they name: `route_ids`: each row names 2 different experts. Among the 64 rows of one device (aligned blocks), no expert is named by more than 48 rows, a bound that some block reaches.
All inputs are finite; a program needn't handle non-finite values.
Results may differ from the reference program's by a relative error of at most 0.015.
Values may be sent and summed in bfloat16 or wider, within the bound.
No kernel may reach another device: no remote copies, remote signals or barrier semaphores. Data moves between devices by JAX's collectives and lax.ppermute only.
A program may use at most 64 MiB of HBM per device.

```python
import math
import jax
import jax.numpy as jnp
import numpy as np
from jax import lax

D = 4096
FF = 1536
RANK = 8
SLOTS = 16
USER_TOK = 8
TOK_DEV = 64
EXPERTS = 4
TOP = 2
CAP = 48
ADAPT = 128
TOKENS = 512
USERS = 64
N_HIDDEN = 2


def place_ends(drawn, key, low, top_value):
    longest = drawn.shape.index(max(drawn.shape))
    spots = []
    for shift in (0, 1):
        where = [jax.random.randint(jax.random.fold_in(key, axis), (), 0, length) for axis, length in enumerate(drawn.shape)]
        where[longest] = (where[longest] + shift) % drawn.shape[longest]
        spots.append(tuple(where))
    return drawn.at[spots[0]].set(low).at[spots[1]].set(top_value)


def block_levels(rng, dims, pieces, smallest, high):
    def one(dim, parts):
        steps = jax.random.uniform(jax.random.fold_in(jax.random.fold_in(rng, 6), dim), (parts,), jnp.float32, smallest / len(pieces), high / len(pieces))
        return jnp.repeat(jnp.exp(steps), dims[dim] // parts).reshape((-1,) + (1,) * (len(dims) - dim - 1))

    factor_of = one(*pieces[0])
    for cut in pieces[1:]:
        factor_of = factor_of * one(*cut)
    return factor_of


def deal_out(key, own, number, rows, count, top, most, lean):
    sequence = jax.random.permutation(key, count)
    heavy_load, common = shares(count, rows * top, most, lean, True), shares(count, rows * top, most, lean, False)
    places = jnp.arange(count)

    def named(lengths, rotation):
        used = int((lengths > 0).sum())
        fixed = max(1, used // 4)
        shifted = fixed + (places - fixed + rotation * (used - fixed)) % max(1, count - fixed)
        return jnp.zeros((count,), jnp.int32).at[sequence[jnp.where(places < fixed, places, shifted)]].set(jnp.asarray(lengths, jnp.int32))

    lengths = jnp.where(number % 4 == 0, named(heavy_load, number // 4), named(common, number - number // 4 - 1))
    mixed = jax.random.permutation(jax.random.fold_in(own, 3), count)
    donor, sink = mixed[0:count // 2 * 2:2], mixed[1:count // 2 * 2:2]
    slack = jnp.minimum(lengths[donor] - 1, most - lengths[sink]) // 2
    slack = jnp.where((donor == sequence[0]) | (sink == sequence[0]) | (lengths[sink] == 0), 0, jnp.maximum(slack, 0))
    shifted = jax.random.randint(jax.random.fold_in(own, 4), (count // 2,), 0, 1 << 20) % (slack + 1)
    lengths = lengths.at[donor].add(-shifted).at[sink].add(shifted)
    labels = jnp.searchsorted(jnp.cumsum(lengths), jnp.arange(rows * top), side="right").astype(jnp.int32)
    table = labels.reshape(top, rows).T
    table = table[jax.random.permutation(jax.random.fold_in(own, 1), rows)]
    rotation = jax.random.randint(jax.random.fold_in(own, 2), (rows, 1), 0, top)
    return jnp.take_along_axis(table, (jnp.arange(top)[None, :] + rotation) % top, axis=1)


def shares(number_of, total, bound, lean, full):
    weights = [(1 << 20) // math.isqrt(standing ** lean) + 1 for standing in range(1, number_of + 1)]
    largest = bound if full else min(bound, max(-(-total // number_of), total * weights[0] // sum(weights)))
    least = 1 if total - largest >= number_of - 1 else 0
    holding, rest = [largest] + [least] * (number_of - 1), total - largest - least * (number_of - 1)
    while rest > 0:
        candidates = [i for i in range(1, number_of) if holding[i] < largest] or [i for i in range(1, number_of) if holding[i] < bound]
        whole, left = sum([weights[i] for i in candidates]), rest
        for i in candidates:
            addition = min(bound - holding[i], max(1, left * weights[i] // whole), rest)
            holding[i] = holding[i] + addition
            rest = rest - addition
    return np.array(holding)


def gaussian(stream_key, shape, scale, bound, shards=(), dtype=jnp.bfloat16):
    level = block_levels(stream_key, shape, shards, -0.22, 0.18) if shards else 1.0
    entries = jax.random.normal(stream_key, shape, jnp.float32) * scale * level
    return jnp.minimum(jnp.maximum(entries, -bound), bound).astype(dtype)


def setup_inputs(seed: int = 0, part: int = 0) -> dict:
    key_list = jax.random.split(jax.random.key(seed), 10)
    own_keys = jax.random.split(jax.random.fold_in(key_list[9], part), 10)
    tokens = gaussian(own_keys[0], (TOKENS, D), 1.0, 6.0, ((0, 8), (1, 2)))
    route_ids_keys = jax.random.split(jax.random.fold_in(own_keys[1], 1), TOKENS // TOK_DEV)
    route_ids_turns = jax.random.permutation(jax.random.fold_in(own_keys[1], 3), TOKENS // TOK_DEV)
    route_ids = jax.vmap(lambda own, number: deal_out(jax.random.fold_in(own_keys[1], 2), own, number, TOK_DEV, EXPERTS, TOP, CAP, 2))(route_ids_keys, route_ids_turns).reshape((TOKENS, TOP))
    route_weight = jnp.clip(0.1 + 0.9 * jax.random.uniform(own_keys[2], (TOKENS, TOP), jnp.float32) ** block_levels(own_keys[2], (TOKENS, TOP), ((0, 8),), -0.2, 0.2), 0.1, 1.0)
    user_slot = place_ends(jax.random.randint(own_keys[3], (USERS, EXPERTS), 0, SLOTS), jax.random.fold_in(own_keys[3], 1), 0, SLOTS - 1).astype(jnp.int32)
    gate_weight = gaussian(key_list[4], (EXPERTS, D, FF), D ** -0.5, 0.09375, ((0, 4), (2, 2)))
    up_weight = gaussian(key_list[5], (EXPERTS, D, FF), D ** -0.5, 0.09375, ((0, 4), (2, 2)))
    down_weight = gaussian(key_list[6], (EXPERTS, FF, D), FF ** -0.5, 0.15625, ((0, 4), (1, 2)))
    adapter_down = gaussian(key_list[7], (EXPERTS, D, ADAPT), D ** -0.5, 0.09375, ((0, 4), (1, 2)))
    adapter_up = gaussian(key_list[8], (EXPERTS, ADAPT, FF), RANK ** -0.5, 2.0, ((0, 4), (2, 2)))
    return {"tokens": tokens, "route_ids": route_ids, "route_weight": route_weight, "user_slot": user_slot, "gate_weight": gate_weight, "up_weight": up_weight, "down_weight": down_weight, "adapter_down": adapter_down, "adapter_up": adapter_up}


def reference(tokens, route_ids, route_weight, user_slot, gate_weight, up_weight, down_weight, adapter_down, adapter_up):
    tokens_count = tokens.shape[0]
    user_of = (jnp.arange(tokens_count) // USER_TOK).astype(jnp.int32)
    slot_table = user_slot[user_of]
    row_positions = jnp.arange(tokens_count)
    group_width = FF // N_HIDDEN

    def per_expert(running, expert_number):
        gate_values = jnp.dot(tokens, gate_weight[expert_number], preferred_element_type=jnp.float32)
        up_values = jnp.dot(tokens, up_weight[expert_number], preferred_element_type=jnp.float32)
        chosen = slot_table[:, expert_number]
        rank_full = jnp.dot(tokens, adapter_down[expert_number], preferred_element_type=jnp.float32)
        rank_portion = rank_full.reshape(tokens_count, SLOTS, RANK)[row_positions, chosen].astype(jnp.bfloat16)
        upward_factor = adapter_up[expert_number].reshape(SLOTS, RANK, FF)[chosen]
        adapter_update = jnp.einsum("xl,xla->xa", rank_portion.astype(jnp.float32), upward_factor.astype(jnp.float32))
        hidden_act = (jax.nn.silu(gate_values) * (up_values + adapter_update)).astype(jnp.bfloat16)
        grouped = hidden_act.reshape(tokens_count, N_HIDDEN, group_width).astype(jnp.float32)
        down_groups = down_weight[expert_number].reshape(N_HIDDEN, group_width, D).astype(jnp.float32)
        partial_value = jnp.einsum("tgf,gfd->tgd", grouped, down_groups).astype(jnp.bfloat16)
        output = jnp.sum(partial_value.astype(jnp.float32), axis=1)
        weight = jnp.sum(jnp.where(route_ids == expert_number, route_weight, 0.0), axis=1)
        return running + weight[:, None] * output, None

    start = jnp.zeros((tokens_count, D), jnp.float32)
    total, _ = lax.scan(per_expert, start, jnp.arange(EXPERTS).astype(jnp.int32))
    return total.astype(jnp.bfloat16)
```

```python
import jax
import jax.numpy as jnp
from jax import lax
from jax.experimental import pallas as pl
from jax.experimental.pallas import tpu as pltpu
from jax.sharding import PartitionSpec as P

RANK = 8
USER_TOK = 8
LIMIT = 12 << 20
VMEM = pl.BlockSpec(memory_space=pltpu.VMEM)
ANY = pl.BlockSpec(memory_space=pl.ANY)
F32 = jnp.float32
BF16 = jnp.bfloat16


def call(body, outs, ins, in_specs=None, scratch=(), flops=0, bytes_=0, aliases=None):
    return pl.pallas_call(
        body,
        out_shape=outs,
        in_specs=in_specs or [VMEM] * len(ins),
        out_specs=[VMEM] * len(outs),
        scratch_shapes=list(scratch),
        input_output_aliases=aliases or {},
        compiler_params=pltpu.CompilerParams(vmem_limit_bytes=LIMIT),
        cost_estimate=pl.CostEstimate(flops=flops, bytes_accessed=bytes_, transcendentals=0),
    )(*ins)


def iota(shape, dim):
    return lax.broadcasted_iota(jnp.int32, shape, dim)


def dot(a, b, dims=((1,), (0,))):
    return lax.dot_general(a, b, (dims, ((), ())), preferred_element_type=F32)


def partner(index, step, count):
    if count & (count - 1) == 0:
        return index ^ step
    return (index + step) % count


def back_partner(index, step, count):
    if count & (count - 1) == 0:
        return index ^ step
    return (index - step + count) % count


def permute(value, axis, step, back=False):
    count = lax.axis_size(axis)
    pairs = [(i, partner(i, step, count)) for i in range(count)]
    if back:
        pairs = [(j, i) for i, j in pairs]
    return lax.ppermute(value, axis, pairs)


def traced_partner(index, step, count):
    if count & (count - 1) == 0:
        return lax.bitwise_xor(index, step)
    return lax.rem(index + step, count)


def traced_back(index, step, count):
    if count & (count - 1) == 0:
        return lax.bitwise_xor(index, step)
    return lax.rem(index - step + count, count)


def routing(ids, experts):
    choices, rows = ids.shape
    padded = -(-experts // 16) * 16
    expert_of = iota((padded, rows), 0)
    chosen = jnp.zeros((padded, rows), F32)
    for k in range(choices):
        chosen = chosen + jnp.where(ids[k : k + 1, :] == expert_of, 1.0, 0.0)
    before = jnp.where(iota((rows, rows), 0) < iota((rows, rows), 1), 1.0, 0.0)
    place = dot(chosen.astype(BF16), before.astype(BF16))
    return expert_of, chosen, place


def row_of(table, expert_of, expert):
    return jnp.sum(jnp.where(expert_of == expert, table, 0.0), axis=0, keepdims=True)


def selection(chosen, place, expert_of, expert, capacity):
    rows = chosen.shape[1]
    hit = row_of(chosen, expert_of, expert)
    at = row_of(place, expert_of, expert)
    return jnp.where((iota((capacity, rows), 0).astype(F32) == at) & (hit > 0.0), 1.0, 0.0)


def local(
    tokens,
    route_ids,
    route_weight,
    user_slot,
    gate_weight,
    up_weight,
    down_weight,
    adapter_down,
    adapter_up,
):
    experts = lax.axis_size("expert")
    hiddens = lax.axis_size("hidden")
    tok_rows, choices = route_ids.shape
    cap = tok_rows * choices * 3 // (2 * experts)
    part = tokens.shape[1]
    half = part // 2
    width = gate_weight.shape[1]
    units = gate_weight.shape[2]
    adapt_cols = adapter_down.shape[2]
    slots = adapt_cols // RANK
    total = experts * cap
    users = user_slot.shape[0]
    steps = sorted(range(1, experts), key=lambda k: (k != experts // 2, k))
    last = steps[-1] if steps else None

    def dispatch(ids, slot, tok, *outs):
        me = lax.axis_index("expert")
        expert_of, chosen, place = routing(ids[...], experts)
        user_at = jnp.where(
            iota((users, tok_rows), 1) // USER_TOK == iota((users, tok_rows), 0), 1.0, 0.0
        )
        slots_of = dot(slot[...].astype(F32).astype(BF16), user_at.astype(BF16))
        picks, index = [], 0
        for k in [0] + steps:
            e = traced_partner(me, k, experts)
            pick = selection(chosen, place, expert_of, e, cap).astype(BF16)
            picks.append(pick)
            own = row_of(slots_of, iota(slots_of.shape, 0), e)
            own = jnp.broadcast_to(own, (8, tok_rows)).astype(BF16)
            outs[index][...] = dot(own, pick, ((1,), (1,)))
            index += 1
        rows = dot(jnp.concatenate(picks, axis=0), tok[...]).astype(BF16)
        for n, k in enumerate([0] + steps):
            piece = rows[n * cap : (n + 1) * cap]
            if k == last:
                outs[index][...] = piece[:, :half]
                outs[index + 1][...] = piece[:, half:]
                index += 2
            else:
                outs[index][...] = piece
                index += 1

    shapes = [jax.ShapeDtypeStruct((8, cap), F32)] * experts
    for k in [0] + steps:
        if k == last:
            shapes += [jax.ShapeDtypeStruct((cap, half), BF16)] * 2
        else:
            shapes += [jax.ShapeDtypeStruct((cap, part), BF16)]
    out = call(dispatch, shapes, (route_ids.T, user_slot.T, tokens))
    codes, pieces = out[:experts], out[experts:]

    def load(*refs):
        n = len(refs) // 2
        sems = refs[-1]
        copies = [
            pltpu.make_async_copy(refs[i], refs[n + i], sems.at[i]) for i in range(n)
        ]
        for c in copies:
            c.start()
        for c in copies:
            c.wait()

    weights = (gate_weight[0], up_weight[0], down_weight[0])
    gate_w, up_w, down_w = pl.pallas_call(
        load,
        out_shape=[pltpu.VMEM(w.shape, w.dtype) for w in weights],
        in_specs=[ANY] * 3,
        out_specs=[VMEM] * 3,
        scratch_shapes=[pltpu.SemaphoreType.DMA((3,))],
        compiler_params=pltpu.CompilerParams(vmem_limit_bytes=4 << 20),
    )(*weights)

    seg_pieces = []
    for k in [0] + steps:
        seg_pieces += [(k, 0, half), (k, half, part)] if k == last else [(k, 0, part)]
    arrived, others = [], [[] for _ in range(hiddens)]
    for (k, lo, hi), piece in zip(seg_pieces, pieces):
        got = piece if k == 0 else permute(piece, "expert", k)
        arrived.append(got)
    got_codes = [codes[0]] + [permute(c, "expert", k) for k, c in zip(steps, codes[1:])]
    for d in range(1, hiddens):
        others[d] = [permute(a, "hidden", d) for a in arrived]

    segments = [(0, half), (half, part)]

    def block(refs, lo, hi, start, size):
        rows = []
        for (k, a, b), ref in zip(seg_pieces, refs):
            if a <= lo and hi <= b:
                rows.append(ref[:, pl.ds(pl.multiple_of(lo - a + start, 128), size)])
        return jnp.concatenate(rows, axis=0)

    n_pieces = len(seg_pieces)

    def multiply(refs, gate_ref, up_ref, acc_gate, acc_up, base):
        for lo, hi in segments:
            tile = min(1024, hi - lo)

            def body(i, _, lo=lo, hi=hi, tile=tile):
                x = block(refs, lo, hi, i * tile, tile)
                at = pl.ds(pl.multiple_of(base + lo + i * tile, 128), tile)
                acc_gate[...] += dot(x, gate_ref[at, :])
                acc_up[...] += dot(x, up_ref[at, :])
                return 0

            if hi - lo == tile:
                body(0, 0)
            else:
                lax.fori_loop(0, (hi - lo) // tile, body, 0)

    def ranks(*refs):
        rows, code, down = refs[:n_pieces], refs[n_pieces : n_pieces + experts], refs[-2]
        out = refs[-1]
        full = jnp.zeros((adapt_cols, total), F32)
        for lo, hi in segments:
            full = full + dot(down[lo:hi, :], block(rows, lo, hi, 0, hi - lo), ((0,), (1,)))
        row_code = jnp.concatenate([c[0:1, :] for c in code], axis=1)
        slot_at = (iota((adapt_cols, total), 0) // RANK).astype(F32)
        kept = jnp.where(slot_at == row_code, full, 0.0)
        out[...] = jnp.sum(kept.reshape(slots, RANK, total), axis=0)

    (rank_part,) = call(
        ranks,
        [jax.ShapeDtypeStruct((RANK, total), F32)],
        (*arrived, *got_codes, adapter_down[0]),
    )
    rank_others = [permute(rank_part, "hidden", d) for d in range(1, hiddens)]

    def first(*refs):
        rows, gate_ref, up_ref, acc_gate, acc_up = refs[:n_pieces], *refs[n_pieces:]
        acc_gate[...] = jnp.zeros_like(acc_gate)
        acc_up[...] = jnp.zeros_like(acc_up)
        base = lax.axis_index("hidden") * part
        multiply(rows, gate_ref, up_ref, acc_gate, acc_up, base)

    acc = [jax.ShapeDtypeStruct((total, units), F32)] * 2
    gate_acc, up_acc = call(first, acc, (*arrived, gate_w, up_w))

    def second(*refs):
        rows = [refs[d * n_pieces : (d + 1) * n_pieces] for d in range(hiddens - 1)]
        rest = refs[(hiddens - 1) * n_pieces :]
        code, rest = rest[:experts], rest[experts:]
        rank_refs, rest = rest[:hiddens], rest[hiddens:]
        gate_in, up_in, gate_ref, up_ref, up_factor, act, acc_gate, acc_up = rest
        h = lax.axis_index("hidden")
        acc_gate[...] = gate_in[...]
        rank = rank_refs[0][...]
        for r in rank_refs[1:]:
            rank = rank + r[...]
        rank = jnp.broadcast_to(rank[None], (slots, RANK, total)).reshape(adapt_cols, total)
        row_code = jnp.concatenate([c[0:1, :] for c in code], axis=1)
        slot_at = (iota((adapt_cols, total), 0) // RANK).astype(F32)
        rank = jnp.where(slot_at == row_code, rank, 0.0).astype(BF16)
        acc_up[...] = up_in[...] + dot(rank, up_factor[...], ((0,), (0,)))
        for d in range(1, hiddens):
            base = traced_back(h, d, hiddens) * part
            multiply(rows[d - 1], gate_ref, up_ref, acc_gate, acc_up, base)
        gate = acc_gate[...]
        act[...] = (gate / (1.0 + jnp.exp(-gate)) * acc_up[...]).astype(BF16)

    (act,) = call(
        second,
        [jax.ShapeDtypeStruct((total, units), BF16)],
        (
            *[a for d in range(1, hiddens) for a in others[d]],
            *got_codes,
            rank_part,
            *rank_others,
            gate_acc,
            up_acc,
            gate_w,
            up_w,
            adapter_up[0],
        ),
        scratch=[pltpu.VMEM((total, units), F32)] * 2,
    )

    def down_cols(act_ref, down_ref, outs, base):
        for lo, hi in segments:
            at = pl.ds(pl.multiple_of(base + lo, 128), hi - lo)
            y = dot(act_ref[...], down_ref[:, at]).astype(BF16)
            n = 0
            for (k, a, b), ref in zip(seg_pieces, outs):
                if a <= lo and hi <= b:
                    ref[:, lo - a : hi - a] = y[n * cap : (n + 1) * cap]
                    n += 1

    piece_shapes = [jax.ShapeDtypeStruct((cap, b - a), BF16) for _, a, b in seg_pieces]

    def down_for(step):
        def body(act_ref, down_ref, *outs):
            h = lax.axis_index("hidden")
            base = traced_partner(h, step, hiddens) * part if step else h * part
            down_cols(act_ref, down_ref, outs, base)

        return call(body, piece_shapes, (act, down_w))

    sent = [down_for(d) for d in range(1, hiddens)]
    kept = down_for(0)
    order = [i for i in reversed(range(n_pieces))]
    if last is not None:
        order = [n_pieces - 2, n_pieces - 1] + [i for i in reversed(range(n_pieces - 2))]
    summed = {}
    for i in order:
        summed[i] = [permute(sent[d - 1][i], "hidden", d) for d in range(1, hiddens)]

    def add(*refs):
        y = refs[0][...].astype(F32)
        for r in refs[1:-1]:
            y = y + r[...].astype(F32)
        refs[-1][...] = y.astype(BF16)

    returned = {}
    for i in order:
        k = seg_pieces[i][0]
        if k == 0:
            continue
        (y,) = call(add, [piece_shapes[i]], (kept[i], *summed[i]))
        returned[i] = permute(y, "expert", k, back=True)

    own_count = hiddens

    def combine(*refs):
        ids, weight = refs[0][...], refs[1][...]
        own, rest, out = refs[2 : 2 + own_count], refs[2 + own_count : -1], refs[-1]
        me = lax.axis_index("expert")
        expert_of, chosen, place = routing(ids, experts)
        weights_of = jnp.zeros(chosen.shape, F32)
        for j in range(choices):
            weights_of = weights_of + jnp.where(ids[j : j + 1] == expert_of, weight[j : j + 1], 0.0)
        mixes = []
        for k in [0] + steps:
            e = traced_partner(me, k, experts)
            pick = selection(chosen, place, expert_of, e, cap)
            mixes.append(pick * row_of(weights_of, expert_of, e))
        mix = jnp.concatenate(mixes, axis=0)
        parts = []
        for _ in range(3):
            piece = mix.astype(BF16)
            parts.append(piece)
            mix = mix - piece.astype(F32)
        for lo, hi in segments:
            y = own[0][:, lo:hi].astype(F32)
            for r in own[1:]:
                y = y + r[:, lo:hi].astype(F32)
            rows = [y.astype(BF16)]
            for (k, a, b), ref in zip(seg_pieces[1:], rest):
                if a <= lo and hi <= b:
                    rows.append(ref[:, lo - a : hi - a])
            rows = jnp.concatenate(rows, axis=0)
            value = dot(parts[0], rows, ((0,), (0,)))
            for piece in parts[1:]:
                value = value + dot(piece, rows, ((0,), (0,)))
            out[:, lo:hi] = value.astype(BF16)

    (mixed,) = call(
        combine,
        [jax.ShapeDtypeStruct((tok_rows, part), BF16)],
        (
            route_ids.T,
            route_weight.T,
            kept[0],
            *summed[0],
            *[returned[i] for i in range(1, n_pieces)],
        ),
    )
    return mixed


def solution(mesh):
    in_specs = (
        P(("parts", "expert", "rep"), "hidden"),
        P(("parts", "expert", "rep"), None),
        P(("parts", "expert", "rep"), None),
        P(("parts", "expert", "rep"), None),
        P("expert", None, "hidden"),
        P("expert", None, "hidden"),
        P("expert", "hidden", None),
        P("expert", "hidden", None),
        P("expert", None, "hidden"),
    )
    out_specs = P(("parts", "expert", "rep"), "hidden")
    return jax.shard_map(local, mesh=mesh, in_specs=in_specs, out_specs=out_specs, check_vma=False)
```

```python
import jax
import jax.numpy as jnp
from jax import lax
from jax.experimental import pallas as pl
from jax.experimental.pallas import tpu as pltpu
from jax.sharding import PartitionSpec as P


RANK = 8
USER_TOK = 8
LANES = 128
ROWS = 16
LIMIT = 12 << 20
VMEM = pl.BlockSpec(memory_space=pltpu.VMEM)
ANY = pl.BlockSpec(memory_space=pl.ANY)
HBM = pl.BlockSpec(memory_space=pltpu.HBM)
F32 = jnp.float32
BF16 = jnp.bfloat16


def call(body, outs, ins, in_specs=None, scratch=(), flops=0):
    return pl.pallas_call(
        body,
        out_shape=outs,
        in_specs=in_specs or [VMEM] * len(ins),
        out_specs=[VMEM] * len(outs),
        scratch_shapes=list(scratch),
        compiler_params=pltpu.CompilerParams(vmem_limit_bytes=LIMIT),
        cost_estimate=pl.CostEstimate(flops=flops, bytes_accessed=flops // 160, transcendentals=0),
    )(*ins)


def iota(shape, dim):
    return lax.broadcasted_iota(jnp.int32, shape, dim)


def dot(a, b, dims=((1,), (0,))):
    return lax.dot_general(a, b, (dims, ((), ())), preferred_element_type=F32)


def swaps(count):
    return count & (count - 1) == 0


def target(index, step, count):
    if swaps(count):
        return index ^ step if isinstance(index, int) else lax.bitwise_xor(index, step)
    return (index + step) % count if isinstance(index, int) else lax.rem(index + step, count)


def source(index, step, count):
    return target(index, step if swaps(count) else count - step, count)


def permute(value, axis, step, back=False):
    count = lax.axis_size(axis)
    pairs = [(i, target(i, step, count)) for i in range(count)]
    if back:
        pairs = [(j, i) for i, j in pairs]
    return lax.ppermute(value, axis, pairs)


def routing(ids, experts):
    choices, rows = ids.shape
    padded = -(-experts // ROWS) * ROWS
    expert_of = iota((padded, rows), 0)
    chosen = jnp.zeros((padded, rows), F32)
    for k in range(choices):
        chosen = chosen + jnp.where(ids[k : k + 1, :] == expert_of, 1.0, 0.0)
    before = jnp.where(iota((rows, rows), 0) < iota((rows, rows), 1), 1.0, 0.0)
    place = dot(chosen.astype(BF16), before.astype(BF16))
    return expert_of, chosen, place


def row_of(table, expert_of, expert):
    return jnp.sum(jnp.where(expert_of == expert, table, 0.0), axis=0, keepdims=True)


def selection(chosen, place, expert_of, expert, capacity):
    rows = chosen.shape[1]
    hit = row_of(chosen, expert_of, expert)
    at = row_of(place, expert_of, expert)
    return jnp.where((iota((capacity, rows), 0).astype(F32) == at) & (hit > 0.0), 1.0, 0.0)


class Piece:
    def __init__(self, step, lo, hi, cap, coded):
        self.step, self.lo, self.hi, self.cap, self.coded = step, lo, hi, cap, coded
        self.across = (hi - lo) // LANES
        self.length = cap * self.across + (ROWS if coded else 0)
        self.shape = jax.ShapeDtypeStruct((self.length, LANES), BF16)

    def covers(self, lo, hi):
        return self.lo <= lo and hi <= self.hi

    def place(self, r, c):
        start = (r * self.across + c) * ROWS
        return slice(start, start + ROWS)

    def store(self, ref, lo, value):
        first = (lo - self.lo) // LANES
        for r in range(self.cap // ROWS):
            for c in range(value.shape[1] // LANES):
                ref[self.place(r, first + c), :] = value[
                    r * ROWS : (r + 1) * ROWS, c * LANES : (c + 1) * LANES
                ]

    def load(self, ref, lo, hi):
        first, last = (lo - self.lo) // LANES, (hi - self.lo) // LANES
        rows = []
        for r in range(self.cap // ROWS):
            tiles = [ref[self.place(r, c), :] for c in range(first, last)]
            rows.append(jnp.concatenate(tiles, axis=1))
        return jnp.concatenate(rows, axis=0)

    def codes(self, ref):
        return ref[self.length - ROWS : self.length, :].astype(F32)[0:1, : self.cap]


def gather(pieces, refs, lo, hi):
    return jnp.concatenate(
        [p.load(r, lo, hi) for p, r in zip(pieces, refs) if p.covers(lo, hi)], axis=0
    )


def local(
    tokens,
    route_ids,
    route_weight,
    user_slot,
    gate_weight,
    up_weight,
    down_weight,
    adapter_down,
    adapter_up,
):
    experts = lax.axis_size("expert")
    hiddens = lax.axis_size("hidden")
    tok_rows, choices = route_ids.shape
    limit = tok_rows * choices * 3 // (2 * experts)
    cap = -(-limit // ROWS) * ROWS
    part = tokens.shape[1]
    half, quarter = part // 2, part // 4
    units = gate_weight.shape[2]
    adapt_cols = adapter_down.shape[2]
    slots = adapt_cols // RANK
    total = experts * cap
    users = user_slot.shape[0]
    steps = list(range(1, experts))
    last = experts - 1
    segments = [(0, half), (half, part)]

    there = []
    for k in range(experts):
        if k and k == last:
            there += [Piece(k, 0, half, cap, True), Piece(k, half, part, cap, False)]
        else:
            there += [Piece(k, 0, part, cap, True)]
    home, first = [], experts // 2
    for k in range(experts):
        if k and k == first:
            home += [Piece(k, 0, quarter, cap, False), Piece(k, quarter, part, cap, False)]
        else:
            home += [Piece(k, 0, part, cap, False)]
    home_segments = [(0, quarter), (quarter, half), (half, part)]
    lead = max(0, min(i for i, p in enumerate(home) if p.step == first))

    def dispatch(ids_in, slot_in, tok_in, *refs):
        *outs, ids, slot, tok, sems = refs
        copies = [
            pltpu.make_async_copy(a, b, sems.at[i])
            for i, (a, b) in enumerate([(ids_in, ids), (slot_in, slot), (tok_in, tok)])
        ]
        for c in copies:
            c.start()
        me = lax.axis_index("expert")
        copies[0].wait()
        copies[1].wait()
        expert_of, chosen, place = routing(ids[...], experts)
        user_at = jnp.where(
            iota((users, tok_rows), 1) // USER_TOK == iota((users, tok_rows), 0), 1.0, 0.0
        )
        slots_of = dot(slot[...].astype(F32).astype(BF16), user_at.astype(BF16))
        picks, codes = [], []
        for k in range(experts):
            e = target(me, k, experts)
            pick = selection(chosen, place, expert_of, e, cap)
            pick = jnp.concatenate([pick, jnp.zeros((LANES - cap, tok_rows), F32)]).astype(BF16)
            own = row_of(slots_of, iota(slots_of.shape, 0), e)
            own = jnp.broadcast_to(own, (ROWS, tok_rows)).astype(BF16)
            codes.append(dot(own, pick, ((1,), (1,))).astype(BF16))
            picks.append(pick[:cap])
        copies[2].wait()
        rows = dot(jnp.concatenate(picks, axis=0), tok[...]).astype(BF16)
        for p, ref in zip(there, outs):
            p.store(ref, p.lo, rows[p.step * cap : (p.step + 1) * cap, p.lo : p.hi])
            if p.coded:
                ref[p.length - ROWS : p.length, :] = codes[p.step]

    sent = call(
        dispatch,
        [p.shape for p in there],
        (route_ids.T, user_slot.T, tokens),
        flops=10**10,
        in_specs=[HBM] * 3,
        scratch=[
            pltpu.VMEM(route_ids.T.shape, jnp.int32),
            pltpu.VMEM(user_slot.T.shape, jnp.int32),
            pltpu.VMEM(tokens.shape, BF16),
            pltpu.SemaphoreType.DMA((3,)),
        ],
    )

    def load(*refs):
        sems = refs[6]
        copies = [pltpu.make_async_copy(refs[i], refs[3 + i], sems.at[i]) for i in range(3)]
        for c in copies:
            c.start()
        for c in copies:
            c.wait()

    weights = (gate_weight[0], up_weight[0], down_weight[0])
    gate_w, up_w, down_w = pl.pallas_call(
        load,
        out_shape=[pltpu.VMEM(w.shape, w.dtype) for w in weights],
        in_specs=[ANY] * 3,
        out_specs=[VMEM] * 3,
        scratch_shapes=[pltpu.SemaphoreType.DMA((3,))],
        compiler_params=pltpu.CompilerParams(vmem_limit_bytes=4 << 20),
        name="load",
    )(*weights)

    arrived = [s if p.step == 0 else permute(s, "expert", p.step) for p, s in zip(there, sent)]
    others = [[permute(a, "hidden", d) for a in arrived] for d in range(1, hiddens)]

    def within(lo, hi, values):
        kept = [i for i, p in enumerate(there) if p.covers(lo, hi)]
        return [there[i] for i in kept], [values[i] for i in kept]

    def multiply(x, gate_ref, up_ref, start):
        at = pl.ds(pl.multiple_of(start, LANES), x.shape[1])
        return dot(x, gate_ref[at, :]), dot(x, up_ref[at, :])

    acc = [jax.ShapeDtypeStruct((total, units), F32)] * 2

    def row_codes(pieces, refs):
        return jnp.concatenate([p.codes(r) for p, r in zip(pieces, refs) if p.coded], axis=1)

    def slot_mask(codes):
        return (iota((adapt_cols, total), 0) // RANK).astype(F32) == codes

    ranks, pieces_a, values_a = None, *within(*segments[0], arrived)
    for s, (lo, hi) in enumerate(segments):
        pieces, values = within(lo, hi, arrived)

        def rank_step(*refs, lo=lo, hi=hi, s=s, pieces=pieces):
            x = gather(pieces, refs, lo, hi)
            full = dot(refs[len(pieces)][lo:hi, :], x, ((0,), (1,)))
            if s:
                full = full + refs[len(pieces) + 1][...]
                codes = row_codes(pieces_a, refs[len(pieces) + 2 :])
                full = jnp.where(slot_mask(codes), full, 0.0)
                full = jnp.sum(full.reshape(slots, RANK, total), axis=0)
            refs[-1][...] = full

        extra = () if ranks is None else (ranks, *values_a)
        shape = (adapt_cols if s == 0 else RANK, total)
        (ranks,) = call(
            rank_step, [jax.ShapeDtypeStruct(shape, F32)], (*values, adapter_down[0], *extra)
        )
    rank_others = [permute(ranks, "hidden", d) for d in range(1, hiddens)]

    sums = None
    for s, (lo, hi) in enumerate(segments):
        pieces, values = within(lo, hi, arrived)

        def own_step(*refs, lo=lo, hi=hi, s=s, pieces=pieces):
            n = len(pieces)
            gate, up = multiply(
                gather(pieces, refs, lo, hi),
                refs[n],
                refs[n + 1],
                lax.axis_index("hidden") * part + lo,
            )
            if s:
                gate, up = gate + refs[n + 2][...], up + refs[n + 3][...]
            refs[-2][...] = gate
            refs[-1][...] = up

        sums = call(own_step, acc, (*values, gate_w, up_w, *(sums or ())))

    def partner_parts(refs, lo, hi, gate_ref, up_ref, gate, up, pieces):
        for d in range(1, hiddens):
            base = source(lax.axis_index("hidden"), d, hiddens) * part + lo
            x = gather(pieces, refs[(d - 1) * len(pieces) : d * len(pieces)], lo, hi)
            g, u = multiply(x, gate_ref, up_ref, base)
            gate, up = gate + g, up + u
        return gate, up

    lo, hi = segments[0]
    pieces = within(lo, hi, there)[0]
    values = [v for o in others for v in within(lo, hi, o)[1]]

    def other_step(*refs):
        gate_ref, up_ref, gate_in, up_in, gate_out, up_out = refs[-6:]
        gate_out[...], up_out[...] = partner_parts(
            refs, *segments[0], gate_ref, up_ref, gate_in[...], up_in[...], pieces_a
        )

    sums = call(other_step, acc, (*values, gate_w, up_w, *sums))

    pieces_b = within(*segments[1], there)[0]
    values = [v for o in others for v in within(*segments[1], o)[1]]

    def store_down(act_rows, down_ref, base, lo, hi, pieces, refs, first):
        at = pl.ds(pl.multiple_of(base + lo, LANES), hi - lo)
        y = dot(act_rows, down_ref[:, at]).astype(BF16)
        for p, ref in zip(pieces, refs):
            if p.covers(lo, hi):
                n = p.step * cap - first
                p.store(ref, lo, y[n : n + cap])

    n_b = len(values)

    def activate(*refs):
        codes = row_codes(pieces_a, refs[n_b : n_b + len(pieces_a)])
        rest = refs[n_b + len(pieces_a) :]
        rank_refs, rest = rest[:hiddens], rest[hiddens:]
        gate_in, up_in, gate_ref, up_ref, factor, down_ref, act_ref = rest[:7]
        rank = rank_refs[0][...]
        for r in rank_refs[1:]:
            rank = rank + r[...]
        rank = jnp.broadcast_to(rank[None], (slots, RANK, total)).reshape(adapt_cols, total)
        rank = jnp.where(slot_mask(codes), rank, 0.0).astype(BF16)
        up = up_in[...] + dot(rank, factor[...], ((0,), (0,)))
        gate, up = partner_parts(
            refs, *segments[1], gate_ref, up_ref, gate_in[...], up, pieces_b
        )
        act = (gate / (1.0 + jnp.exp(-gate)) * up).astype(BF16)
        act_ref[...] = act
        p = home[lead]
        for d in range(1, hiddens):
            base = target(lax.axis_index("hidden"), d, hiddens) * part
            rows = act[p.step * cap : (p.step + 1) * cap]
            store_down(rows, down_ref, base, p.lo, p.hi, [p], [rest[6 + d]], p.step * cap)
        base = lax.axis_index("hidden") * part
        store_down(rows, down_ref, base, p.lo, p.hi, [p], [rest[-1]], p.step * cap)

    act, *lead_sent, lead_kept = call(
        activate,
        [jax.ShapeDtypeStruct((total, units), BF16)] + [home[lead].shape] * hiddens,
        (
            *values,
            *within(*segments[0], arrived)[1],
            ranks,
            *rank_others,
            *sums,
            gate_w,
            up_w,
            adapter_up[0],
            down_w,
        ),
    )

    def down(step, pieces):
        def body(act_ref, down_ref, *outs):
            base = target(lax.axis_index("hidden"), step, hiddens) * part if step else (
                lax.axis_index("hidden") * part
            )
            for lo, hi in home_segments:
                if any(p.covers(lo, hi) for p in pieces):
                    store_down(act_ref[...], down_ref, base, lo, hi, pieces, outs, 0)

        return call(body, [p.shape for p in pieces], (act, down_w))

    rest = [i for i in range(len(home)) if i != lead]
    sent_home = []
    for d in range(1, hiddens):
        out = down(d, [home[i] for i in rest])
        sent_home.append({lead: lead_sent[d - 1], **dict(zip(rest, out))})
    kept = {lead: lead_kept, **dict(zip(rest, down(0, [home[i] for i in rest])))}
    order = [lead] + ([lead + 1] if lead else [])
    order += [i for i in reversed(range(len(home))) if i not in order]
    summed = {
        i: [permute(sent_home[d - 1][i], "hidden", d) for d in range(1, hiddens)]
        for i in order
    }

    def add(*refs):
        y = refs[0][...].astype(F32)
        for r in refs[1:-1]:
            y = y + r[...].astype(F32)
        refs[-1][...] = y.astype(BF16)

    returned = {}
    for i in order:
        if home[i].step:
            (y,) = call(add, [home[i].shape], (kept[i], *summed[i]))
            returned[i] = permute(y, "expert", home[i].step, back=True)

    final = max([i for i in range(len(home)) if home[i].step not in (0, first)], default=0)
    early = [i for i in range(len(home)) if home[i].step and i != final]

    def mixing(ids, weight, chosen_steps):
        me = lax.axis_index("expert")
        expert_of, chosen, place = routing(ids, experts)
        weights_of = jnp.zeros(chosen.shape, F32)
        for j in range(choices):
            weights_of = weights_of + jnp.where(ids[j : j + 1] == expert_of, weight[j : j + 1], 0.0)
        mix = []
        for k in chosen_steps:
            e = target(me, k, experts)
            mix.append(
                selection(chosen, place, expert_of, e, cap) * row_of(weights_of, expert_of, e)
            )
        mix = jnp.concatenate(mix, axis=0)
        terms = []
        for _ in range(3):
            terms.append(mix.astype(BF16))
            mix = mix - terms[-1].astype(F32)
        return terms

    def mixed_sum(terms, rows):
        value = dot(terms[0], rows, ((0,), (0,)))
        for t in terms[1:]:
            value = value + dot(t, rows, ((0,), (0,)))
        return value

    early_steps = [0] + [k for k in steps if any(home[i].step == k for i in early)]

    def combine(*refs):
        own, others_in = refs[2 : 2 + hiddens], refs[2 + hiddens : -4]
        terms = mixing(refs[0][...], refs[1][...], early_steps)
        for lo, hi in home_segments:
            y = home[0].load(own[0], lo, hi).astype(F32)
            for r in own[1:]:
                y = y + home[0].load(r, lo, hi).astype(F32)
            rows = [y.astype(BF16)]
            rows += [
                home[i].load(r, lo, hi) for i, r in zip(early, others_in) if home[i].covers(lo, hi)
            ]
            refs[-4][:, lo:hi] = mixed_sum(terms, jnp.concatenate(rows, axis=0))
        for ref, t in zip(refs[-3:], mixing(refs[0][...], refs[1][...], [home[final].step])):
            ref[...] = t

    mixed, *final_terms = call(
        combine,
        [jax.ShapeDtypeStruct((tok_rows, part), F32)]
        + [jax.ShapeDtypeStruct((cap, tok_rows), BF16)] * 3,
        (route_ids.T, route_weight.T, kept[0], *summed[0], *[returned[i] for i in early]),
    )

    def finish(partial, *refs):
        terms, out = [r[...] for r in refs[:3]], refs[-1]
        for lo, hi in home_segments:
            value = partial[:, lo:hi]
            if final:
                value = value + mixed_sum(terms, home[final].load(refs[3], lo, hi))
            out[:, lo:hi] = value.astype(BF16)

    (result,) = call(
        finish,
        [jax.ShapeDtypeStruct((tok_rows, part), BF16)],
        (mixed, *final_terms, *([returned[final]] if final else [])),
    )
    return result


def solution(mesh):
    in_specs = (
        P(("parts", "expert", "rep"), "hidden"),
        P(("parts", "expert", "rep"), None),
        P(("parts", "expert", "rep"), None),
        P(("parts", "expert", "rep"), None),
        P("expert", None, "hidden"),
        P("expert", None, "hidden"),
        P("expert", "hidden", None),
        P("expert", "hidden", None),
        P("expert", None, "hidden"),
    )
    out_specs = P(("parts", "expert", "rep"), "hidden")

    return jax.shard_map(local, mesh=mesh, in_specs=in_specs, out_specs=out_specs, check_vma=False)
```

```python
import jax
import jax.numpy as jnp
from jax import lax
from jax.experimental import pallas as pl
from jax.experimental.pallas import tpu as pltpu
from jax.sharding import PartitionSpec as P


RANK = 8
USER_TOK = 8
LANES = 128
ROWS = 16
LIMIT = 12 << 20
VMEM = pl.BlockSpec(memory_space=pltpu.VMEM)
ANY = pl.BlockSpec(memory_space=pl.ANY)
HBM = pl.BlockSpec(memory_space=pltpu.HBM)
F32 = jnp.float32
BF16 = jnp.bfloat16


def call(body, outs, ins, in_specs=None, scratch=(), flops=0):
    return pl.pallas_call(
        body,
        out_shape=outs,
        in_specs=in_specs or [VMEM] * len(ins),
        out_specs=[VMEM] * len(outs),
        scratch_shapes=list(scratch),
        compiler_params=pltpu.CompilerParams(vmem_limit_bytes=LIMIT),
        cost_estimate=pl.CostEstimate(flops=flops, bytes_accessed=flops // 160, transcendentals=0),
    )(*ins)


def iota(shape, dim):
    return lax.broadcasted_iota(jnp.int32, shape, dim)


def dot(a, b, dims=((1,), (0,))):
    return lax.dot_general(a, b, (dims, ((), ())), preferred_element_type=F32)


def swaps(count):
    return count & (count - 1) == 0


def target(index, step, count):
    if swaps(count):
        return index ^ step if isinstance(index, int) else lax.bitwise_xor(index, step)
    return (index + step) % count if isinstance(index, int) else lax.rem(index + step, count)


def source(index, step, count):
    return target(index, step if swaps(count) else count - step, count)


def permute(value, axis, step, back=False):
    count = lax.axis_size(axis)
    pairs = [(i, target(i, step, count)) for i in range(count)]
    if back:
        pairs = [(j, i) for i, j in pairs]
    return lax.ppermute(value, axis, pairs)


def routing(ids, experts):
    choices, rows = ids.shape
    padded = -(-experts // ROWS) * ROWS
    expert_of = iota((padded, rows), 0)
    chosen = jnp.zeros((padded, rows), F32)
    for k in range(choices):
        chosen = chosen + jnp.where(ids[k : k + 1, :] == expert_of, 1.0, 0.0)
    before = jnp.where(iota((rows, rows), 0) < iota((rows, rows), 1), 1.0, 0.0)
    place = dot(chosen.astype(BF16), before.astype(BF16))
    return expert_of, chosen, place


def row_of(table, expert_of, expert):
    return jnp.sum(jnp.where(expert_of == expert, table, 0.0), axis=0, keepdims=True)


def selection(chosen, place, expert_of, expert, capacity):
    rows = chosen.shape[1]
    hit = row_of(chosen, expert_of, expert)
    at = row_of(place, expert_of, expert)
    return jnp.where((iota((capacity, rows), 0).astype(F32) == at) & (hit > 0.0), 1.0, 0.0)


class Piece:
    def __init__(self, step, lo, hi, cap, coded):
        self.step, self.lo, self.hi, self.cap, self.coded = step, lo, hi, cap, coded
        self.across = (hi - lo) // LANES
        self.length = cap * self.across + (ROWS if coded else 0)
        self.shape = jax.ShapeDtypeStruct((self.length, LANES), BF16)

    def covers(self, lo, hi):
        return self.lo <= lo and hi <= self.hi

    def place(self, r, c):
        start = (r * self.across + c) * ROWS
        return slice(start, start + ROWS)

    def store(self, ref, lo, value):
        first = (lo - self.lo) // LANES
        for r in range(self.cap // ROWS):
            for c in range(value.shape[1] // LANES):
                ref[self.place(r, first + c), :] = value[
                    r * ROWS : (r + 1) * ROWS, c * LANES : (c + 1) * LANES
                ]

    def load(self, ref, lo, hi):
        first, last = (lo - self.lo) // LANES, (hi - self.lo) // LANES
        rows = []
        for r in range(self.cap // ROWS):
            tiles = [ref[self.place(r, c), :] for c in range(first, last)]
            rows.append(jnp.concatenate(tiles, axis=1))
        return jnp.concatenate(rows, axis=0)

    def codes(self, ref):
        return ref[self.length - ROWS : self.length, :].astype(F32)[0:1, : self.cap]


def gather(pieces, refs, lo, hi):
    return jnp.concatenate(
        [p.load(r, lo, hi) for p, r in zip(pieces, refs) if p.covers(lo, hi)], axis=0
    )


def local(
    tokens,
    route_ids,
    route_weight,
    user_slot,
    gate_weight,
    up_weight,
    down_weight,
    adapter_down,
    adapter_up,
):
    experts = lax.axis_size("expert")
    hiddens = lax.axis_size("hidden")
    tok_rows, choices = route_ids.shape
    limit = tok_rows * choices * 3 // (2 * experts)
    cap = -(-limit // ROWS) * ROWS
    part = tokens.shape[1]
    half, quarter = part // 2, part // 4
    units = gate_weight.shape[2]
    adapt_cols = adapter_down.shape[2]
    slots = adapt_cols // RANK
    total = experts * cap
    users = user_slot.shape[0]
    steps = list(range(1, experts))
    last = experts - 1
    segments = [(0, half), (half, part)]

    there = []
    for k in range(experts):
        if k and k in (1, last):
            there += [Piece(k, 0, half, cap, True), Piece(k, half, part, cap, False)]
        else:
            there += [Piece(k, 0, part, cap, True)]
    home, first = [], experts // 2
    for k in range(experts):
        if k and k == first:
            home += [Piece(k, 0, quarter, cap, False), Piece(k, quarter, part, cap, False)]
        else:
            home += [Piece(k, 0, part, cap, False)]
    home_segments = [(0, quarter), (quarter, half), (half, part)]
    lead = max(0, min(i for i, p in enumerate(home) if p.step == first))

    def dispatch(ids_in, slot_in, tok_in, *refs):
        *outs, ids, slot, tok, sems = refs
        copies = [
            pltpu.make_async_copy(a, b, sems.at[i])
            for i, (a, b) in enumerate([(ids_in, ids), (slot_in, slot), (tok_in, tok)])
        ]
        for c in copies:
            c.start()
        me = lax.axis_index("expert")
        copies[0].wait()
        copies[1].wait()
        expert_of, chosen, place = routing(ids[...], experts)
        user_at = jnp.where(
            iota((users, tok_rows), 1) // USER_TOK == iota((users, tok_rows), 0), 1.0, 0.0
        )
        slots_of = dot(slot[...].astype(F32).astype(BF16), user_at.astype(BF16))
        picks, codes = [], []
        for k in range(experts):
            e = target(me, k, experts)
            pick = selection(chosen, place, expert_of, e, cap)
            pick = jnp.concatenate([pick, jnp.zeros((LANES - cap, tok_rows), F32)]).astype(BF16)
            own = row_of(slots_of, iota(slots_of.shape, 0), e)
            own = jnp.broadcast_to(own, (ROWS, tok_rows)).astype(BF16)
            codes.append(dot(own, pick, ((1,), (1,))).astype(BF16))
            picks.append(pick[:cap])
        copies[2].wait()
        rows = dot(jnp.concatenate(picks, axis=0), tok[...]).astype(BF16)
        for p, ref in zip(there, outs):
            p.store(ref, p.lo, rows[p.step * cap : (p.step + 1) * cap, p.lo : p.hi])
            if p.coded:
                ref[p.length - ROWS : p.length, :] = codes[p.step]

    sent = call(
        dispatch,
        [p.shape for p in there],
        tuple(pltpu.with_memory_space_constraint(v, pltpu.HBM) for v in (route_ids.T, user_slot.T, tokens)),
        in_specs=[HBM] * 3,
        scratch=[
            pltpu.VMEM(route_ids.T.shape, jnp.int32),
            pltpu.VMEM(user_slot.T.shape, jnp.int32),
            pltpu.VMEM(tokens.shape, BF16),
            pltpu.SemaphoreType.DMA((3,)),
        ],
    )

    def pace(inp, out):
        out[...] = inp[...]

    sent = [*call(pace, [there[0].shape], (sent[0],), flops=10**10), *sent[1:]]

    def load(*refs):
        sems = refs[6]
        copies = [pltpu.make_async_copy(refs[i], refs[3 + i], sems.at[i]) for i in range(3)]
        for c in copies:
            c.start()
        for c in copies:
            c.wait()

    weights = (gate_weight[0], up_weight[0], down_weight[0])
    gate_w, up_w, down_w = pl.pallas_call(
        load,
        out_shape=[pltpu.VMEM(w.shape, w.dtype) for w in weights],
        in_specs=[ANY] * 3,
        out_specs=[VMEM] * 3,
        scratch_shapes=[pltpu.SemaphoreType.DMA((3,))],
        compiler_params=pltpu.CompilerParams(vmem_limit_bytes=4 << 20),
        name="load",
    )(*weights)

    arrived = [s if p.step == 0 else permute(s, "expert", p.step) for p, s in zip(there, sent)]
    others = [[permute(a, "hidden", d) for a in arrived] for d in range(1, hiddens)]

    def within(lo, hi, values):
        kept = [i for i, p in enumerate(there) if p.covers(lo, hi)]
        return [there[i] for i in kept], [values[i] for i in kept]

    def multiply(x, gate_ref, up_ref, start):
        at = pl.ds(pl.multiple_of(start, LANES), x.shape[1])
        return dot(x, gate_ref[at, :]), dot(x, up_ref[at, :])

    acc = [jax.ShapeDtypeStruct((total, units), F32)] * 2

    def row_codes(pieces, refs):
        return jnp.concatenate([p.codes(r) for p, r in zip(pieces, refs) if p.coded], axis=1)

    def slot_mask(codes):
        return (iota((adapt_cols, total), 0) // RANK).astype(F32) == codes

    ranks, pieces_a, values_a = None, *within(*segments[0], arrived)
    for s, (lo, hi) in enumerate(segments):
        pieces, values = within(lo, hi, arrived)

        def rank_step(*refs, lo=lo, hi=hi, s=s, pieces=pieces):
            x = gather(pieces, refs, lo, hi)
            full = dot(refs[len(pieces)][lo:hi, :], x, ((0,), (1,)))
            if s:
                full = full + refs[len(pieces) + 1][...]
                codes = row_codes(pieces_a, refs[len(pieces) + 2 :])
                full = jnp.where(slot_mask(codes), full, 0.0)
                full = jnp.sum(full.reshape(slots, RANK, total), axis=0)
            refs[-1][...] = full

        extra = () if ranks is None else (ranks, *values_a)
        shape = (adapt_cols if s == 0 else RANK, total)
        (ranks,) = call(
            rank_step, [jax.ShapeDtypeStruct(shape, F32)], (*values, adapter_down[0], *extra)
        )
    rank_others = [permute(ranks, "hidden", d) for d in range(1, hiddens)]

    sums = None
    for s, (lo, hi) in enumerate(segments):
        pieces, values = within(lo, hi, arrived)

        def own_step(*refs, lo=lo, hi=hi, s=s, pieces=pieces):
            n = len(pieces)
            gate, up = multiply(
                gather(pieces, refs, lo, hi),
                refs[n],
                refs[n + 1],
                lax.axis_index("hidden") * part + lo,
            )
            if s:
                gate, up = gate + refs[n + 2][...], up + refs[n + 3][...]
            refs[-2][...] = gate
            refs[-1][...] = up

        sums = call(own_step, acc, (*values, gate_w, up_w, *(sums or ())))

    def partner_parts(refs, lo, hi, gate_ref, up_ref, gate, up, pieces):
        for d in range(1, hiddens):
            base = source(lax.axis_index("hidden"), d, hiddens) * part + lo
            x = gather(pieces, refs[(d - 1) * len(pieces) : d * len(pieces)], lo, hi)
            g, u = multiply(x, gate_ref, up_ref, base)
            gate, up = gate + g, up + u
        return gate, up

    lo, hi = segments[0]
    pieces = within(lo, hi, there)[0]
    values = [v for o in others for v in within(lo, hi, o)[1]]

    def other_step(*refs):
        gate_ref, up_ref, gate_in, up_in, gate_out, up_out = refs[-6:]
        gate_out[...], up_out[...] = partner_parts(
            refs, *segments[0], gate_ref, up_ref, gate_in[...], up_in[...], pieces_a
        )

    sums = call(other_step, acc, (*values, gate_w, up_w, *sums))

    pieces_b = within(*segments[1], there)[0]
    values = [v for o in others for v in within(*segments[1], o)[1]]

    def store_down(act_rows, down_ref, base, lo, hi, pieces, refs, first):
        at = pl.ds(pl.multiple_of(base + lo, LANES), hi - lo)
        y = dot(act_rows, down_ref[:, at]).astype(BF16)
        for p, ref in zip(pieces, refs):
            if p.covers(lo, hi):
                n = p.step * cap - first
                p.store(ref, lo, y[n : n + cap])

    n_b = len(values)

    def activate(*refs):
        codes = row_codes(pieces_a, refs[n_b : n_b + len(pieces_a)])
        rest = refs[n_b + len(pieces_a) :]
        rank_refs, rest = rest[:hiddens], rest[hiddens:]
        gate_in, up_in, gate_ref, up_ref, factor, down_ref, act_ref = rest[:7]
        rank = rank_refs[0][...]
        for r in rank_refs[1:]:
            rank = rank + r[...]
        rank = jnp.broadcast_to(rank[None], (slots, RANK, total)).reshape(adapt_cols, total)
        rank = jnp.where(slot_mask(codes), rank, 0.0).astype(BF16)
        up = up_in[...] + dot(rank, factor[...], ((0,), (0,)))
        gate, up = partner_parts(
            refs, *segments[1], gate_ref, up_ref, gate_in[...], up, pieces_b
        )
        act = (gate / (1.0 + jnp.exp(-gate)) * up).astype(BF16)
        act_ref[...] = act
        p = home[lead]
        for d in range(1, hiddens):
            base = target(lax.axis_index("hidden"), d, hiddens) * part
            rows = act[p.step * cap : (p.step + 1) * cap]
            store_down(rows, down_ref, base, p.lo, p.hi, [p], [rest[6 + d]], p.step * cap)
        base = lax.axis_index("hidden") * part
        store_down(rows, down_ref, base, p.lo, p.hi, [p], [rest[-1]], p.step * cap)

    act, *lead_sent, lead_kept = call(
        activate,
        [jax.ShapeDtypeStruct((total, units), BF16)] + [home[lead].shape] * hiddens,
        (
            *values,
            *within(*segments[0], arrived)[1],
            ranks,
            *rank_others,
            *sums,
            gate_w,
            up_w,
            adapter_up[0],
            down_w,
        ),
    )

    def down(step, pieces):
        def body(act_ref, down_ref, *outs):
            base = target(lax.axis_index("hidden"), step, hiddens) * part if step else (
                lax.axis_index("hidden") * part
            )
            for lo, hi in home_segments:
                if any(p.covers(lo, hi) for p in pieces):
                    store_down(act_ref[...], down_ref, base, lo, hi, pieces, outs, 0)

        return call(body, [p.shape for p in pieces], (act, down_w))

    rest = [i for i in range(len(home)) if i != lead]
    sent_home = []
    for d in range(1, hiddens):
        out = down(d, [home[i] for i in rest])
        sent_home.append({lead: lead_sent[d - 1], **dict(zip(rest, out))})
    kept = {lead: lead_kept, **dict(zip(rest, down(0, [home[i] for i in rest])))}
    order = [lead] + ([lead + 1] if lead else [])
    order += [i for i in reversed(range(len(home))) if i not in order]
    summed = {
        i: [permute(sent_home[d - 1][i], "hidden", d) for d in range(1, hiddens)]
        for i in order
    }

    def add(*refs):
        y = refs[0][...].astype(F32)
        for r in refs[1:-1]:
            y = y + r[...].astype(F32)
        refs[-1][...] = y.astype(BF16)

    returned = {}
    for i in order:
        if home[i].step:
            (y,) = call(add, [home[i].shape], (kept[i], *summed[i]))
            returned[i] = permute(y, "expert", home[i].step, back=True)

    final = max([i for i in range(len(home)) if home[i].step not in (0, first)], default=0)
    early = [i for i in range(len(home)) if home[i].step and i != final]

    def mixing(ids, weight, chosen_steps):
        me = lax.axis_index("expert")
        expert_of, chosen, place = routing(ids, experts)
        weights_of = jnp.zeros(chosen.shape, F32)
        for j in range(choices):
            weights_of = weights_of + jnp.where(ids[j : j + 1] == expert_of, weight[j : j + 1], 0.0)
        mix = []
        for k in chosen_steps:
            e = target(me, k, experts)
            mix.append(
                selection(chosen, place, expert_of, e, cap) * row_of(weights_of, expert_of, e)
            )
        mix = jnp.concatenate(mix, axis=0)
        terms = []
        for _ in range(3):
            terms.append(mix.astype(BF16))
            mix = mix - terms[-1].astype(F32)
        return terms

    def mixed_sum(terms, rows):
        value = dot(terms[0], rows, ((0,), (0,)))
        for t in terms[1:]:
            value = value + dot(t, rows, ((0,), (0,)))
        return value

    early_steps = [0] + [k for k in steps if any(home[i].step == k for i in early)]

    def combine(*refs):
        own, others_in = refs[2 : 2 + hiddens], refs[2 + hiddens : -4]
        terms = mixing(refs[0][...], refs[1][...], early_steps)
        for lo, hi in home_segments:
            y = home[0].load(own[0], lo, hi).astype(F32)
            for r in own[1:]:
                y = y + home[0].load(r, lo, hi).astype(F32)
            rows = [y.astype(BF16)]
            rows += [
                home[i].load(r, lo, hi) for i, r in zip(early, others_in) if home[i].covers(lo, hi)
            ]
            refs[-4][:, lo:hi] = mixed_sum(terms, jnp.concatenate(rows, axis=0))
        for ref, t in zip(refs[-3:], mixing(refs[0][...], refs[1][...], [home[final].step])):
            ref[...] = t

    mixed, *final_terms = call(
        combine,
        [jax.ShapeDtypeStruct((tok_rows, part), F32)]
        + [jax.ShapeDtypeStruct((cap, tok_rows), BF16)] * 3,
        (route_ids.T, route_weight.T, kept[0], *summed[0], *[returned[i] for i in early]),
    )

    def finish(partial, *refs):
        terms, out = [r[...] for r in refs[:3]], refs[-1]
        for lo, hi in home_segments:
            value = partial[:, lo:hi]
            if final:
                value = value + mixed_sum(terms, home[final].load(refs[3], lo, hi))
            out[:, lo:hi] = value.astype(BF16)

    (result,) = call(
        finish,
        [jax.ShapeDtypeStruct((tok_rows, part), BF16)],
        (mixed, *final_terms, *([returned[final]] if final else [])),
    )
    return result


def solution(mesh):
    in_specs = (
        P(("parts", "expert", "rep"), "hidden"),
        P(("parts", "expert", "rep"), None),
        P(("parts", "expert", "rep"), None),
        P(("parts", "expert", "rep"), None),
        P("expert", None, "hidden"),
        P("expert", None, "hidden"),
        P("expert", "hidden", None),
        P("expert", "hidden", None),
        P("expert", None, "hidden"),
    )
    out_specs = P(("parts", "expert", "rep"), "hidden")

    return jax.shard_map(local, mesh=mesh, in_specs=in_specs, out_specs=out_specs, check_vma=False)
```

```python
import jax
import jax.numpy as jnp
from jax import lax
from jax.experimental import pallas as pl
from jax.experimental.pallas import tpu as pltpu
from jax.sharding import PartitionSpec as P


RANK = 8
USER_TOK = 8
LANES = 128
ROWS = 16
LIMIT = 12 << 20
VMEM = pl.BlockSpec(memory_space=pltpu.VMEM)
ANY = pl.BlockSpec(memory_space=pl.ANY)
HBM = pl.BlockSpec(memory_space=pltpu.HBM)
F32 = jnp.float32
BF16 = jnp.bfloat16


def call(body, outs, ins, in_specs=None, scratch=(), flops=0, out_specs=None):
    return pl.pallas_call(
        body,
        out_shape=outs,
        in_specs=in_specs or [VMEM] * len(ins),
        out_specs=out_specs or [VMEM] * len(outs),
        scratch_shapes=list(scratch),
        compiler_params=pltpu.CompilerParams(vmem_limit_bytes=LIMIT),
        cost_estimate=pl.CostEstimate(flops=flops, bytes_accessed=flops // 160, transcendentals=0),
    )(*ins)


def iota(shape, dim):
    return lax.broadcasted_iota(jnp.int32, shape, dim)


def dot(a, b, dims=((1,), (0,))):
    return lax.dot_general(a, b, (dims, ((), ())), preferred_element_type=F32)


def swaps(count):
    return count & (count - 1) == 0


def target(index, step, count):
    if swaps(count):
        return index ^ step if isinstance(index, int) else lax.bitwise_xor(index, step)
    return (index + step) % count if isinstance(index, int) else lax.rem(index + step, count)


def source(index, step, count):
    return target(index, step if swaps(count) else count - step, count)


def permute(value, axis, step, back=False):
    count = lax.axis_size(axis)
    pairs = [(i, target(i, step, count)) for i in range(count)]
    if back:
        pairs = [(j, i) for i, j in pairs]
    return lax.ppermute(value, axis, pairs)


def routing(ids, experts):
    choices, rows = ids.shape
    padded = -(-experts // ROWS) * ROWS
    expert_of = iota((padded, rows), 0)
    chosen = jnp.zeros((padded, rows), F32)
    for k in range(choices):
        chosen = chosen + jnp.where(ids[k : k + 1, :] == expert_of, 1.0, 0.0)
    before = jnp.where(iota((rows, rows), 0) < iota((rows, rows), 1), 1.0, 0.0)
    place = dot(chosen.astype(BF16), before.astype(BF16))
    return expert_of, chosen, place


def row_of(table, expert_of, expert):
    return jnp.sum(jnp.where(expert_of == expert, table, 0.0), axis=0, keepdims=True)


def selection(chosen, place, expert_of, expert, capacity):
    rows = chosen.shape[1]
    hit = row_of(chosen, expert_of, expert)
    at = row_of(place, expert_of, expert)
    return jnp.where((iota((capacity, rows), 0).astype(F32) == at) & (hit > 0.0), 1.0, 0.0)


class Piece:
    def __init__(self, step, lo, hi, cap, coded):
        self.step, self.lo, self.hi, self.cap, self.coded = step, lo, hi, cap, coded
        self.across = (hi - lo) // LANES
        self.length = cap * self.across + (ROWS if coded else 0)
        self.shape = jax.ShapeDtypeStruct((self.length, LANES), BF16)

    def covers(self, lo, hi):
        return self.lo <= lo and hi <= self.hi

    def place(self, r, c):
        start = (r * self.across + c) * ROWS
        return slice(start, start + ROWS)

    def store(self, ref, lo, value):
        first = (lo - self.lo) // LANES
        for r in range(self.cap // ROWS):
            for c in range(value.shape[1] // LANES):
                ref[self.place(r, first + c), :] = value[
                    r * ROWS : (r + 1) * ROWS, c * LANES : (c + 1) * LANES
                ]

    def load(self, ref, lo, hi):
        first, last = (lo - self.lo) // LANES, (hi - self.lo) // LANES
        rows = []
        for r in range(self.cap // ROWS):
            tiles = [ref[self.place(r, c), :] for c in range(first, last)]
            rows.append(jnp.concatenate(tiles, axis=1))
        return jnp.concatenate(rows, axis=0)

    def codes(self, ref):
        return ref[self.length - ROWS : self.length, :].astype(F32)[0:1, : self.cap]


def gather(pieces, refs, lo, hi):
    return jnp.concatenate(
        [p.load(r, lo, hi) for p, r in zip(pieces, refs) if p.covers(lo, hi)], axis=0
    )


def local(
    tokens,
    route_ids,
    route_weight,
    user_slot,
    gate_weight,
    up_weight,
    down_weight,
    adapter_down,
    adapter_up,
):
    experts = lax.axis_size("expert")
    hiddens = lax.axis_size("hidden")
    tok_rows, choices = route_ids.shape
    limit = tok_rows * choices * 3 // (2 * experts)
    cap = -(-limit // ROWS) * ROWS
    part = tokens.shape[1]
    half, quarter = part // 2, part // 4
    units = gate_weight.shape[2]
    adapt_cols = adapter_down.shape[2]
    slots = adapt_cols // RANK
    total = experts * cap
    users = user_slot.shape[0]
    steps = list(range(1, experts))
    last = experts - 1
    segments = [(0, half), (half, part)]

    there = []
    for k in range(experts):
        if k and k in (1, last):
            there += [Piece(k, 0, half, cap, True), Piece(k, half, part, cap, False)]
        else:
            there += [Piece(k, 0, part, cap, True)]
    home, first = [], experts // 2
    for k in range(experts):
        if k and k == first:
            home += [Piece(k, 0, quarter, cap, False), Piece(k, quarter, part, cap, False)]
        else:
            home += [Piece(k, 0, part, cap, False)]
    home_segments = [(0, quarter), (quarter, half), (half, part)]
    lead = max(0, min(i for i, p in enumerate(home) if p.step == first))

    def dispatch(ids_in, slot_in, tok_in, *refs):
        *outs, ids, slot, tok, sems = refs
        copies = [
            pltpu.make_async_copy(a, b, sems.at[i])
            for i, (a, b) in enumerate([(ids_in, ids), (slot_in, slot), (tok_in, tok)])
        ]
        for c in copies:
            c.start()
        me = lax.axis_index("expert")
        copies[0].wait()
        copies[1].wait()
        expert_of, chosen, place = routing(ids[...], experts)
        user_at = jnp.where(
            iota((users, tok_rows), 1) // USER_TOK == iota((users, tok_rows), 0), 1.0, 0.0
        )
        slots_of = dot(slot[...].astype(F32).astype(BF16), user_at.astype(BF16))
        picks, codes = [], []
        for k in range(experts):
            e = target(me, k, experts)
            pick = selection(chosen, place, expert_of, e, cap)
            pick = jnp.concatenate([pick, jnp.zeros((LANES - cap, tok_rows), F32)]).astype(BF16)
            own = row_of(slots_of, iota(slots_of.shape, 0), e)
            own = jnp.broadcast_to(own, (ROWS, tok_rows)).astype(BF16)
            codes.append(dot(own, pick, ((1,), (1,))).astype(BF16))
            picks.append(pick[:cap])
        copies[2].wait()
        rows = dot(jnp.concatenate(picks, axis=0), tok[...]).astype(BF16)
        for p, ref in zip(there, outs):
            p.store(ref, p.lo, rows[p.step * cap : (p.step + 1) * cap, p.lo : p.hi])
            if p.coded:
                ref[p.length - ROWS : p.length, :] = codes[p.step]

    sent = call(
        dispatch,
        [p.shape for p in there],
        tuple(pltpu.with_memory_space_constraint(v, pltpu.HBM) for v in (route_ids.T, user_slot.T, tokens)),
        in_specs=[HBM] * 3,
        scratch=[
            pltpu.VMEM(route_ids.T.shape, jnp.int32),
            pltpu.VMEM(user_slot.T.shape, jnp.int32),
            pltpu.VMEM(tokens.shape, BF16),
            pltpu.SemaphoreType.DMA((3,)),
        ],
    )

    def pace(inp, out):
        out[...] = inp[...]

    sent = [*call(pace, [there[0].shape], (sent[0],), flops=10**10), *sent[1:]]

    def load(*refs):
        sems = refs[6]
        copies = [pltpu.make_async_copy(refs[i], refs[3 + i], sems.at[i]) for i in range(3)]
        for c in copies:
            c.start()
        for c in copies:
            c.wait()

    weights = (gate_weight[0], up_weight[0], down_weight[0])
    gate_w, up_w, down_w = pl.pallas_call(
        load,
        out_shape=[pltpu.VMEM(w.shape, w.dtype) for w in weights],
        in_specs=[ANY] * 3,
        out_specs=[VMEM] * 3,
        scratch_shapes=[pltpu.SemaphoreType.DMA((3,))],
        compiler_params=pltpu.CompilerParams(vmem_limit_bytes=4 << 20),
        name="load",
    )(*weights)

    arrived = [s if p.step == 0 else permute(s, "expert", p.step) for p, s in zip(there, sent)]
    others = [[permute(a, "hidden", d) for a in arrived] for d in range(1, hiddens)]

    def within(lo, hi, values):
        kept = [i for i, p in enumerate(there) if p.covers(lo, hi)]
        return [there[i] for i in kept], [values[i] for i in kept]

    def multiply(x, gate_ref, up_ref, start):
        at = pl.ds(pl.multiple_of(start, LANES), x.shape[1])
        return dot(x, gate_ref[at, :]), dot(x, up_ref[at, :])

    acc = [jax.ShapeDtypeStruct((total, units), F32)] * 2

    def row_codes(pieces, refs):
        return jnp.concatenate([p.codes(r) for p, r in zip(pieces, refs) if p.coded], axis=1)

    def slot_mask(codes):
        return (iota((adapt_cols, total), 0) // RANK).astype(F32) == codes

    ranks, pieces_a, values_a = None, *within(*segments[0], arrived)
    for s, (lo, hi) in enumerate(segments):
        pieces, values = within(lo, hi, arrived)

        def rank_step(*refs, lo=lo, hi=hi, s=s, pieces=pieces):
            x = gather(pieces, refs, lo, hi)
            full = dot(refs[len(pieces)][lo:hi, :], x, ((0,), (1,)))
            if s:
                full = full + refs[len(pieces) + 1][...]
                codes = row_codes(pieces_a, refs[len(pieces) + 2 :])
                full = jnp.where(slot_mask(codes), full, 0.0)
                full = jnp.sum(full.reshape(slots, RANK, total), axis=0)
            refs[-1][...] = full

        extra = () if ranks is None else (ranks, *values_a)
        shape = (adapt_cols if s == 0 else RANK, total)
        (ranks,) = call(
            rank_step, [jax.ShapeDtypeStruct(shape, F32)], (*values, adapter_down[0], *extra)
        )
    rank_others = [permute(ranks, "hidden", d) for d in range(1, hiddens)]

    sums = None
    for s, (lo, hi) in enumerate(segments):
        pieces, values = within(lo, hi, arrived)

        def own_step(*refs, lo=lo, hi=hi, s=s, pieces=pieces):
            n = len(pieces)
            gate, up = multiply(
                gather(pieces, refs, lo, hi),
                refs[n],
                refs[n + 1],
                lax.axis_index("hidden") * part + lo,
            )
            if s:
                gate, up = gate + refs[n + 2][...], up + refs[n + 3][...]
            refs[-2][...] = gate
            refs[-1][...] = up

        sums = call(own_step, acc, (*values, gate_w, up_w, *(sums or ())))

    def partner_parts(refs, lo, hi, gate_ref, up_ref, gate, up, pieces):
        for d in range(1, hiddens):
            base = source(lax.axis_index("hidden"), d, hiddens) * part + lo
            x = gather(pieces, refs[(d - 1) * len(pieces) : d * len(pieces)], lo, hi)
            g, u = multiply(x, gate_ref, up_ref, base)
            gate, up = gate + g, up + u
        return gate, up

    lo, hi = segments[0]
    pieces = within(lo, hi, there)[0]
    values = [v for o in others for v in within(lo, hi, o)[1]]

    def other_step(*refs):
        gate_ref, up_ref, gate_in, up_in, gate_out, up_out = refs[-6:]
        gate_out[...], up_out[...] = partner_parts(
            refs, *segments[0], gate_ref, up_ref, gate_in[...], up_in[...], pieces_a
        )

    sums = call(other_step, acc, (*values, gate_w, up_w, *sums))

    pieces_b = within(*segments[1], there)[0]
    values = [v for o in others for v in within(*segments[1], o)[1]]

    def store_down(act_rows, down_ref, base, lo, hi, pieces, refs, first):
        at = pl.ds(pl.multiple_of(base + lo, LANES), hi - lo)
        y = dot(act_rows, down_ref[:, at]).astype(BF16)
        for p, ref in zip(pieces, refs):
            if p.covers(lo, hi):
                n = p.step * cap - first
                p.store(ref, lo, y[n : n + cap])

    n_b = len(values)

    def activate(*refs):
        codes = row_codes(pieces_a, refs[n_b : n_b + len(pieces_a)])
        rest = refs[n_b + len(pieces_a) :]
        rank_refs, rest = rest[:hiddens], rest[hiddens:]
        gate_in, up_in, gate_ref, up_ref, factor, down_ref, act_ref = rest[:7]
        rank = rank_refs[0][...]
        for r in rank_refs[1:]:
            rank = rank + r[...]
        rank = jnp.broadcast_to(rank[None], (slots, RANK, total)).reshape(adapt_cols, total)
        rank = jnp.where(slot_mask(codes), rank, 0.0).astype(BF16)
        up = up_in[...] + dot(rank, factor[...], ((0,), (0,)))
        gate, up = partner_parts(
            refs, *segments[1], gate_ref, up_ref, gate_in[...], up, pieces_b
        )
        act = (gate / (1.0 + jnp.exp(-gate)) * up).astype(BF16)
        act_ref[...] = act
        p = home[lead]
        for d in range(1, hiddens):
            base = target(lax.axis_index("hidden"), d, hiddens) * part
            rows = act[p.step * cap : (p.step + 1) * cap]
            store_down(rows, down_ref, base, p.lo, p.hi, [p], [rest[6 + d]], p.step * cap)
        base = lax.axis_index("hidden") * part
        store_down(rows, down_ref, base, p.lo, p.hi, [p], [rest[-1]], p.step * cap)

    act, *lead_sent, lead_kept = call(
        activate,
        [jax.ShapeDtypeStruct((total, units), BF16)] + [home[lead].shape] * hiddens,
        (
            *values,
            *within(*segments[0], arrived)[1],
            ranks,
            *rank_others,
            *sums,
            gate_w,
            up_w,
            adapter_up[0],
            down_w,
        ),
    )

    def down(step, pieces):
        def body(act_ref, down_ref, *outs):
            base = target(lax.axis_index("hidden"), step, hiddens) * part if step else (
                lax.axis_index("hidden") * part
            )
            for lo, hi in home_segments:
                if any(p.covers(lo, hi) for p in pieces):
                    store_down(act_ref[...], down_ref, base, lo, hi, pieces, outs, 0)

        return call(body, [p.shape for p in pieces], (act, down_w))

    rest = [i for i in range(len(home)) if i != lead]
    sent_home = []
    for d in range(1, hiddens):
        out = down(d, [home[i] for i in rest])
        sent_home.append({lead: lead_sent[d - 1], **dict(zip(rest, out))})
    kept = {lead: lead_kept, **dict(zip(rest, down(0, [home[i] for i in rest])))}
    order = [lead] + ([lead + 1] if lead else [])
    order += [i for i in reversed(range(len(home))) if i not in order]
    summed = {
        i: [permute(sent_home[d - 1][i], "hidden", d) for d in range(1, hiddens)]
        for i in order
    }

    def add(*refs):
        y = refs[0][...].astype(F32)
        for r in refs[1:-1]:
            y = y + r[...].astype(F32)
        refs[-1][...] = y.astype(BF16)

    returned = {}
    for i in order:
        if home[i].step:
            (y,) = call(add, [home[i].shape], (kept[i], *summed[i]))
            returned[i] = permute(y, "expert", home[i].step, back=True)

    final = max([i for i in range(len(home)) if home[i].step not in (0, first)], default=0)
    early = [i for i in range(len(home)) if home[i].step and i != final]

    def mixing(ids, weight, chosen_steps):
        me = lax.axis_index("expert")
        expert_of, chosen, place = routing(ids, experts)
        weights_of = jnp.zeros(chosen.shape, F32)
        for j in range(choices):
            weights_of = weights_of + jnp.where(ids[j : j + 1] == expert_of, weight[j : j + 1], 0.0)
        mix = []
        for k in chosen_steps:
            e = target(me, k, experts)
            mix.append(
                selection(chosen, place, expert_of, e, cap) * row_of(weights_of, expert_of, e)
            )
        mix = jnp.concatenate(mix, axis=0)
        terms = []
        for _ in range(3):
            terms.append(mix.astype(BF16))
            mix = mix - terms[-1].astype(F32)
        return terms

    def mixed_sum(terms, rows):
        value = dot(terms[0], rows, ((0,), (0,)))
        for t in terms[1:]:
            value = value + dot(t, rows, ((0,), (0,)))
        return value

    early_steps = [0] + [k for k in steps if any(home[i].step == k for i in early)]

    def combine(*refs):
        own, others_in = refs[2 : 2 + hiddens], refs[2 + hiddens : -4]
        terms = mixing(refs[0][...], refs[1][...], early_steps)
        for lo, hi in home_segments:
            y = home[0].load(own[0], lo, hi).astype(F32)
            for r in own[1:]:
                y = y + home[0].load(r, lo, hi).astype(F32)
            rows = [y.astype(BF16)]
            rows += [
                home[i].load(r, lo, hi) for i, r in zip(early, others_in) if home[i].covers(lo, hi)
            ]
            n = len(rows) * cap
            rows = jnp.concatenate(rows, axis=0)
            refs[-4][:, lo:hi] = mixed_sum([t[:n] for t in terms], rows)
        for ref, t in zip(refs[-3:], mixing(refs[0][...], refs[1][...], [home[final].step])):
            ref[...] = t

    mixed, *final_terms = call(
        combine,
        [jax.ShapeDtypeStruct((tok_rows, part), F32)]
        + [jax.ShapeDtypeStruct((cap, tok_rows), BF16)] * 3,
        (route_ids.T, route_weight.T, kept[0], *summed[0], *[returned[i] for i in early]),
    )

    def finish(partial, *refs):
        terms, out, staged, sems = [r[...] for r in refs[:3]], refs[-3], refs[-2], refs[-1]
        copies = []
        for i, (lo, hi) in enumerate(home_segments):
            value = partial[:, lo:hi]
            if final and home[final].covers(lo, hi):
                value = value + mixed_sum(terms, home[final].load(refs[3], lo, hi))
            staged[:, lo:hi] = value.astype(BF16)
            copies.append(
                pltpu.make_async_copy(staged.at[:, lo:hi], out.at[:, lo:hi], sems.at[i])
            )
            copies[-1].start()
        for c in copies:
            c.wait()

    (result,) = call(
        finish,
        [jax.ShapeDtypeStruct((tok_rows, part), BF16)],
        (mixed, *final_terms, *([returned[final]] if final else [])),
        out_specs=[ANY],
        scratch=[
            pltpu.VMEM((tok_rows, part), BF16),
            pltpu.SemaphoreType.DMA((len(home_segments),)),
        ],
    )
    return result


def solution(mesh):
    in_specs = (
        P(("parts", "expert", "rep"), "hidden"),
        P(("parts", "expert", "rep"), None),
        P(("parts", "expert", "rep"), None),
        P(("parts", "expert", "rep"), None),
        P("expert", None, "hidden"),
        P("expert", None, "hidden"),
        P("expert", "hidden", None),
        P("expert", "hidden", None),
        P("expert", None, "hidden"),
    )
    out_specs = P(("parts", "expert", "rep"), "hidden")

    return jax.shard_map(local, mesh=mesh, in_specs=in_specs, out_specs=out_specs, check_vma=False)
```

```python
import jax
import jax.numpy as jnp
from jax import lax
from jax.experimental import pallas as pl
from jax.experimental.pallas import tpu as pltpu
from jax.sharding import PartitionSpec as P


RANK = 8
USER_TOK = 8
LANES = 128
ROWS = 16
LIMIT = 12 << 20
VMEM = pl.BlockSpec(memory_space=pltpu.VMEM)
ANY = pl.BlockSpec(memory_space=pl.ANY)
HBM = pl.BlockSpec(memory_space=pltpu.HBM)
F32 = jnp.float32
BF16 = jnp.bfloat16


def call(body, outs, ins, in_specs=None, scratch=(), flops=0, out_specs=None):
    return pl.pallas_call(
        body,
        out_shape=outs,
        in_specs=in_specs or [VMEM] * len(ins),
        out_specs=out_specs or [VMEM] * len(outs),
        scratch_shapes=list(scratch),
        compiler_params=pltpu.CompilerParams(vmem_limit_bytes=LIMIT),
        cost_estimate=pl.CostEstimate(flops=flops, bytes_accessed=flops // 160, transcendentals=0),
    )(*ins)


def iota(shape, dim):
    return lax.broadcasted_iota(jnp.int32, shape, dim)


def dot(a, b, dims=((1,), (0,))):
    return lax.dot_general(a, b, (dims, ((), ())), preferred_element_type=F32)


def swaps(count):
    return count & (count - 1) == 0


def target(index, step, count):
    if swaps(count):
        return index ^ step if isinstance(index, int) else lax.bitwise_xor(index, step)
    return (index + step) % count if isinstance(index, int) else lax.rem(index + step, count)


def source(index, step, count):
    return target(index, step if swaps(count) else count - step, count)


def permute(value, axis, step, back=False):
    count = lax.axis_size(axis)
    pairs = [(i, target(i, step, count)) for i in range(count)]
    if back:
        pairs = [(j, i) for i, j in pairs]
    return lax.ppermute(value, axis, pairs)


def routing(ids, experts):
    choices, rows = ids.shape
    padded = -(-experts // ROWS) * ROWS
    expert_of = iota((padded, rows), 0)
    chosen = jnp.zeros((padded, rows), F32)
    for k in range(choices):
        chosen = chosen + jnp.where(ids[k : k + 1, :] == expert_of, 1.0, 0.0)
    before = jnp.where(iota((rows, rows), 0) < iota((rows, rows), 1), 1.0, 0.0)
    place = dot(chosen.astype(BF16), before.astype(BF16))
    return expert_of, chosen, place


def row_of(table, expert_of, expert):
    return jnp.sum(jnp.where(expert_of == expert, table, 0.0), axis=0, keepdims=True)


def selection(chosen, place, expert_of, expert, capacity):
    rows = chosen.shape[1]
    hit = row_of(chosen, expert_of, expert)
    at = row_of(place, expert_of, expert)
    return jnp.where((iota((capacity, rows), 0).astype(F32) == at) & (hit > 0.0), 1.0, 0.0)


class Piece:
    def __init__(self, step, lo, hi, cap, coded):
        self.step, self.lo, self.hi, self.cap, self.coded = step, lo, hi, cap, coded
        self.across = (hi - lo) // LANES
        self.length = cap * self.across + (ROWS if coded else 0)
        self.shape = jax.ShapeDtypeStruct((self.length, LANES), BF16)

    def covers(self, lo, hi):
        return self.lo <= lo and hi <= self.hi

    def place(self, r, c):
        start = (r * self.across + c) * ROWS
        return slice(start, start + ROWS)

    def store(self, ref, lo, value):
        first = (lo - self.lo) // LANES
        for r in range(self.cap // ROWS):
            for c in range(value.shape[1] // LANES):
                ref[self.place(r, first + c), :] = value[
                    r * ROWS : (r + 1) * ROWS, c * LANES : (c + 1) * LANES
                ]

    def load(self, ref, lo, hi):
        first, last = (lo - self.lo) // LANES, (hi - self.lo) // LANES
        rows = []
        for r in range(self.cap // ROWS):
            tiles = [ref[self.place(r, c), :] for c in range(first, last)]
            rows.append(jnp.concatenate(tiles, axis=1))
        return jnp.concatenate(rows, axis=0)

    def codes(self, ref):
        return ref[self.length - ROWS : self.length, :].astype(F32)[0:1, : self.cap]


def gather(pieces, refs, lo, hi):
    return jnp.concatenate(
        [p.load(r, lo, hi) for p, r in zip(pieces, refs) if p.covers(lo, hi)], axis=0
    )


def local(
    tokens,
    route_ids,
    route_weight,
    user_slot,
    gate_weight,
    up_weight,
    down_weight,
    adapter_down,
    adapter_up,
):
    experts = lax.axis_size("expert")
    hiddens = lax.axis_size("hidden")
    tok_rows, choices = route_ids.shape
    limit = tok_rows * choices * 3 // (2 * experts)
    cap = -(-limit // ROWS) * ROWS
    part = tokens.shape[1]
    half, quarter = part // 2, part // 4
    units = gate_weight.shape[2]
    adapt_cols = adapter_down.shape[2]
    slots = adapt_cols // RANK
    total = experts * cap
    users = user_slot.shape[0]
    steps = list(range(1, experts))
    last = experts - 1
    segments = [(0, half), (half, part)]

    there = []
    for k in range(experts):
        if k and k in (1, last):
            there += [Piece(k, 0, half, cap, True), Piece(k, half, part, cap, False)]
        else:
            there += [Piece(k, 0, part, cap, True)]
    home, first = [], experts // 2
    for k in range(experts):
        if k and k == first:
            home += [Piece(k, 0, half, cap, False), Piece(k, half, part, cap, False)]
        else:
            home += [Piece(k, 0, part, cap, False)]
    home_segments = [(0, quarter), (quarter, half), (half, part)]
    lead = max(0, min(i for i, p in enumerate(home) if p.step == first))

    def dispatch(ids_in, slot_in, tok_in, *refs):
        *outs, ids, slot, tok, sems = refs
        copies = [
            pltpu.make_async_copy(a, b, sems.at[i])
            for i, (a, b) in enumerate([(ids_in, ids), (slot_in, slot), (tok_in, tok)])
        ]
        for c in copies:
            c.start()
        me = lax.axis_index("expert")
        copies[0].wait()
        copies[1].wait()
        expert_of, chosen, place = routing(ids[...], experts)
        user_at = jnp.where(
            iota((users, tok_rows), 1) // USER_TOK == iota((users, tok_rows), 0), 1.0, 0.0
        )
        slots_of = dot(slot[...].astype(F32).astype(BF16), user_at.astype(BF16))
        picks, codes = [], []
        for k in range(experts):
            e = target(me, k, experts)
            pick = selection(chosen, place, expert_of, e, cap)
            pick = jnp.concatenate([pick, jnp.zeros((LANES - cap, tok_rows), F32)]).astype(BF16)
            own = row_of(slots_of, iota(slots_of.shape, 0), e)
            own = jnp.broadcast_to(own, (ROWS, tok_rows)).astype(BF16)
            codes.append(dot(own, pick, ((1,), (1,))).astype(BF16))
            picks.append(pick[:cap])
        copies[2].wait()
        rows = dot(jnp.concatenate(picks, axis=0), tok[...]).astype(BF16)
        for p, ref in zip(there, outs):
            p.store(ref, p.lo, rows[p.step * cap : (p.step + 1) * cap, p.lo : p.hi])
            if p.coded:
                ref[p.length - ROWS : p.length, :] = codes[p.step]

    sent = call(
        dispatch,
        [p.shape for p in there],
        tuple(pltpu.with_memory_space_constraint(v, pltpu.HBM) for v in (route_ids.T, user_slot.T, tokens)),
        in_specs=[HBM] * 3,
        scratch=[
            pltpu.VMEM(route_ids.T.shape, jnp.int32),
            pltpu.VMEM(user_slot.T.shape, jnp.int32),
            pltpu.VMEM(tokens.shape, BF16),
            pltpu.SemaphoreType.DMA((3,)),
        ],
    )

    def pace(inp, out):
        out[...] = inp[...]

    sent = [*call(pace, [there[0].shape], (sent[0],), flops=10**10), *sent[1:]]

    def load(*refs):
        sems = refs[6]
        copies = [pltpu.make_async_copy(refs[i], refs[3 + i], sems.at[i]) for i in range(3)]
        for c in copies:
            c.start()
        for c in copies:
            c.wait()

    weights = (gate_weight[0], up_weight[0], down_weight[0])
    gate_w, up_w, down_w = pl.pallas_call(
        load,
        out_shape=[pltpu.VMEM(w.shape, w.dtype) for w in weights],
        in_specs=[ANY] * 3,
        out_specs=[VMEM] * 3,
        scratch_shapes=[pltpu.SemaphoreType.DMA((3,))],
        compiler_params=pltpu.CompilerParams(vmem_limit_bytes=4 << 20),
        name="load",
    )(*weights)

    arrived = [s if p.step == 0 else permute(s, "expert", p.step) for p, s in zip(there, sent)]
    others = [[permute(a, "hidden", d) for a in arrived] for d in range(1, hiddens)]

    def within(lo, hi, values):
        kept = [i for i, p in enumerate(there) if p.covers(lo, hi)]
        return [there[i] for i in kept], [values[i] for i in kept]

    def multiply(x, gate_ref, up_ref, start):
        at = pl.ds(pl.multiple_of(start, LANES), x.shape[1])
        return dot(x, gate_ref[at, :]), dot(x, up_ref[at, :])

    acc = [jax.ShapeDtypeStruct((total, units), F32)] * 2

    def row_codes(pieces, refs):
        return jnp.concatenate([p.codes(r) for p, r in zip(pieces, refs) if p.coded], axis=1)

    def slot_mask(codes):
        return (iota((adapt_cols, total), 0) // RANK).astype(F32) == codes

    ranks, pieces_a, values_a = None, *within(*segments[0], arrived)
    for s, (lo, hi) in enumerate(segments):
        pieces, values = within(lo, hi, arrived)

        def rank_step(*refs, lo=lo, hi=hi, s=s, pieces=pieces):
            x = gather(pieces, refs, lo, hi)
            full = dot(refs[len(pieces)][lo:hi, :], x, ((0,), (1,)))
            if s:
                full = full + refs[len(pieces) + 1][...]
                codes = row_codes(pieces_a, refs[len(pieces) + 2 :])
                full = jnp.where(slot_mask(codes), full, 0.0)
                full = jnp.sum(full.reshape(slots, RANK, total), axis=0)
            refs[-1][...] = full

        extra = () if ranks is None else (ranks, *values_a)
        shape = (adapt_cols if s == 0 else RANK, total)
        (ranks,) = call(
            rank_step, [jax.ShapeDtypeStruct(shape, F32)], (*values, adapter_down[0], *extra)
        )
    rank_others = [permute(ranks, "hidden", d) for d in range(1, hiddens)]

    sums = None
    for s, (lo, hi) in enumerate(segments):
        pieces, values = within(lo, hi, arrived)

        def own_step(*refs, lo=lo, hi=hi, s=s, pieces=pieces):
            n = len(pieces)
            gate, up = multiply(
                gather(pieces, refs, lo, hi),
                refs[n],
                refs[n + 1],
                lax.axis_index("hidden") * part + lo,
            )
            if s:
                gate, up = gate + refs[n + 2][...], up + refs[n + 3][...]
            refs[-2][...] = gate
            refs[-1][...] = up

        sums = call(own_step, acc, (*values, gate_w, up_w, *(sums or ())))

    def partner_parts(refs, lo, hi, gate_ref, up_ref, gate, up, pieces):
        for d in range(1, hiddens):
            base = source(lax.axis_index("hidden"), d, hiddens) * part + lo
            x = gather(pieces, refs[(d - 1) * len(pieces) : d * len(pieces)], lo, hi)
            g, u = multiply(x, gate_ref, up_ref, base)
            gate, up = gate + g, up + u
        return gate, up

    lo, hi = segments[0]
    pieces = within(lo, hi, there)[0]
    values = [v for o in others for v in within(lo, hi, o)[1]]

    def other_step(*refs):
        gate_ref, up_ref, gate_in, up_in, gate_out, up_out = refs[-6:]
        gate_out[...], up_out[...] = partner_parts(
            refs, *segments[0], gate_ref, up_ref, gate_in[...], up_in[...], pieces_a
        )

    sums = call(other_step, acc, (*values, gate_w, up_w, *sums))

    pieces_b = within(*segments[1], there)[0]
    values = [v for o in others for v in within(*segments[1], o)[1]]

    def store_down(act_rows, down_ref, base, lo, hi, pieces, refs, first):
        at = pl.ds(pl.multiple_of(base + lo, LANES), hi - lo)
        y = dot(act_rows, down_ref[:, at]).astype(BF16)
        for p, ref in zip(pieces, refs):
            if p.covers(lo, hi):
                n = p.step * cap - first
                p.store(ref, lo, y[n : n + cap])

    n_b = len(values)

    def activate(*refs):
        codes = row_codes(pieces_a, refs[n_b : n_b + len(pieces_a)])
        rest = refs[n_b + len(pieces_a) :]
        rank_refs, rest = rest[:hiddens], rest[hiddens:]
        gate_in, up_in, gate_ref, up_ref, factor, down_ref, act_ref = rest[:7]
        rank = rank_refs[0][...]
        for r in rank_refs[1:]:
            rank = rank + r[...]
        rank = jnp.broadcast_to(rank[None], (slots, RANK, total)).reshape(adapt_cols, total)
        rank = jnp.where(slot_mask(codes), rank, 0.0).astype(BF16)
        up = up_in[...] + dot(rank, factor[...], ((0,), (0,)))
        gate, up = partner_parts(
            refs, *segments[1], gate_ref, up_ref, gate_in[...], up, pieces_b
        )
        act = (gate / (1.0 + jnp.exp(-gate)) * up).astype(BF16)
        act_ref[...] = act
        p = home[lead]
        for d in range(1, hiddens):
            base = target(lax.axis_index("hidden"), d, hiddens) * part
            rows = act[p.step * cap : (p.step + 1) * cap]
            store_down(rows, down_ref, base, p.lo, p.hi, [p], [rest[6 + d]], p.step * cap)

    act, *lead_sent = call(
        activate,
        [jax.ShapeDtypeStruct((total, units), BF16)] + [home[lead].shape] * (hiddens - 1),
        (
            *values,
            *within(*segments[0], arrived)[1],
            ranks,
            *rank_others,
            *sums,
            gate_w,
            up_w,
            adapter_up[0],
            down_w,
        ),
    )

    def down(step, pieces, lead_too=False):
        def body(act_ref, down_ref, *outs):
            if lead_too:
                p = home[lead]
                rows = act_ref[p.step * cap : (p.step + 1) * cap, :]
                base = lax.axis_index("hidden") * part
                store_down(rows, down_ref, base, p.lo, p.hi, [p], outs[-1:], p.step * cap)
            base = target(lax.axis_index("hidden"), step, hiddens) * part if step else (
                lax.axis_index("hidden") * part
            )
            for lo, hi in home_segments:
                if any(p.covers(lo, hi) for p in pieces):
                    store_down(act_ref[...], down_ref, base, lo, hi, pieces, outs, 0)

        shapes = [p.shape for p in pieces] + [home[lead].shape] * lead_too
        return call(body, shapes, (act, down_w))

    rest = [i for i in range(len(home)) if i != lead]
    sent_home = []
    for d in range(1, hiddens):
        out = down(d, [home[i] for i in rest], d == 1)
        if d == 1:
            *out, lead_kept = out
        sent_home.append({lead: lead_sent[d - 1], **dict(zip(rest, out))})
    kept = {lead: lead_kept, **dict(zip(rest, down(0, [home[i] for i in rest])))}
    order = [lead] + ([lead + 1] if lead else [])
    order += [i for i in reversed(range(len(home))) if i not in order]
    summed = {
        i: [permute(sent_home[d - 1][i], "hidden", d) for d in range(1, hiddens)]
        for i in order
        if home[i].step > 1
    }

    def add(*refs):
        y = refs[0][...].astype(F32)
        for r in refs[1:-1]:
            y = y + r[...].astype(F32)
        refs[-1][...] = y.astype(BF16)

    returned = {}
    for i in order:
        if home[i].step > 1:
            (y,) = call(add, [home[i].shape], (kept[i], *summed[i]))
            returned[i] = permute(y, "expert", home[i].step, back=True)

    final = max([i for i in range(len(home)) if home[i].step not in (0, first)], default=0)
    early = [i for i in range(len(home)) if home[i].step > 1 and i != final]

    def mixing(ids, weight, chosen_steps):
        me = lax.axis_index("expert")
        expert_of, chosen, place = routing(ids, experts)
        weights_of = jnp.zeros(chosen.shape, F32)
        for j in range(choices):
            weights_of = weights_of + jnp.where(ids[j : j + 1] == expert_of, weight[j : j + 1], 0.0)
        mix = []
        for k in chosen_steps:
            e = target(me, k, experts)
            mix.append(
                selection(chosen, place, expert_of, e, cap) * row_of(weights_of, expert_of, e)
            )
        mix = jnp.concatenate(mix, axis=0)
        terms = []
        for _ in range(3):
            terms.append(mix.astype(BF16))
            mix = mix - terms[-1].astype(F32)
        return terms

    def mixed_sum(terms, rows):
        value = dot(jnp.concatenate(terms, axis=1), rows, ((0,), (0,)))
        return value[:tok_rows] + value[tok_rows : 2 * tok_rows] + value[2 * tok_rows :]

    early_steps = [k for k in steps if any(home[i].step == k for i in early)]
    tokens_tile = Piece(None, 0, part, tok_rows, False)

    near = [0, 1]
    near_parts = [[kept[i] for i in near]]
    near_parts += [[sent_home[d - 1][i] for i in near] for d in range(1, hiddens)]
    near_parts = [[own, permute(row, "expert", 1, back=True)] for own, row in near_parts]

    def near_mix(ids, weight, *refs):
        terms = mixing(ids[...], weight[...], near)
        for d in range(hiddens):
            own, row = refs[2 * d : 2 * d + 2]
            for lo, hi in segments:
                rows = jnp.concatenate(
                    [home[0].load(own, lo, hi), home[1].load(row, lo, hi)], axis=0
                )
                value = mixed_sum(terms, rows)
                if d:
                    tokens_tile.store(refs[2 * hiddens + d], lo, value.astype(BF16))
                else:
                    refs[2 * hiddens][:, lo:hi] = value

    near_kept, *near_away = call(
        near_mix,
        [jax.ShapeDtypeStruct((tok_rows, part), F32)] + [tokens_tile.shape] * (hiddens - 1),
        (route_ids.T, route_weight.T, *[v for pair in near_parts for v in pair]),
    )
    near_others = [permute(near_away[d - 1], "hidden", d) for d in range(1, hiddens)]

    def combine(*refs):
        terms = mixing(refs[0][...], refs[1][...], early_steps)
        for lo, hi in home_segments:
            rows = [home[i].load(r, lo, hi) for i, r in zip(early, refs[2:]) if home[i].covers(lo, hi)]
            refs[-4][:, lo:hi] = mixed_sum(terms, jnp.concatenate(rows, axis=0))
        for ref, t in zip(refs[-3:], mixing(refs[0][...], refs[1][...], [home[final].step])):
            ref[...] = t

    mixed, *final_terms = call(
        combine,
        [jax.ShapeDtypeStruct((tok_rows, part), F32)]
        + [jax.ShapeDtypeStruct((cap, tok_rows), BF16)] * 3,
        (route_ids.T, route_weight.T, *[returned[i] for i in early]),
    )

    def finish(partial, kept_sum, *refs):
        terms, refs = [r[...] for r in refs[:3]], refs[3:]
        row, others_in = refs[0], refs[1:hiddens]
        out, staged, sems = refs[-3:]
        copies = []
        for i, (lo, hi) in enumerate(home_segments):
            value = partial[:, lo:hi] + kept_sum[:, lo:hi]
            for r in others_in:
                value = value + tokens_tile.load(r, lo, hi).astype(F32)
            value = value + mixed_sum(terms, home[final].load(row, lo, hi))
            staged[:, lo:hi] = value.astype(BF16)
            copies.append(
                pltpu.make_async_copy(staged.at[:, lo:hi], out.at[:, lo:hi], sems.at[i])
            )
            copies[-1].start()
        for c in copies:
            c.wait()

    (result,) = call(
        finish,
        [jax.ShapeDtypeStruct((tok_rows, part), BF16)],
        (mixed, near_kept, *final_terms, returned[final], *near_others),
        out_specs=[ANY],
        scratch=[
            pltpu.VMEM((tok_rows, part), BF16),
            pltpu.SemaphoreType.DMA((len(home_segments),)),
        ],
    )
    return result


def solution(mesh):
    in_specs = (
        P(("parts", "expert", "rep"), "hidden"),
        P(("parts", "expert", "rep"), None),
        P(("parts", "expert", "rep"), None),
        P(("parts", "expert", "rep"), None),
        P("expert", None, "hidden"),
        P("expert", None, "hidden"),
        P("expert", "hidden", None),
        P("expert", "hidden", None),
        P("expert", None, "hidden"),
    )
    out_specs = P(("parts", "expert", "rep"), "hidden")

    return jax.shard_map(local, mesh=mesh, in_specs=in_specs, out_specs=out_specs, check_vma=False)
```

```python
import jax
import jax.numpy as jnp
from jax import lax
from jax.experimental import pallas as pl
from jax.experimental.pallas import tpu as pltpu
from jax.sharding import PartitionSpec as P


RANK = 8
USER_TOK = 8
LANES = 128
ROWS = 16
LIMIT = 12 << 20
VMEM = pl.BlockSpec(memory_space=pltpu.VMEM)
ANY = pl.BlockSpec(memory_space=pl.ANY)
HBM = pl.BlockSpec(memory_space=pltpu.HBM)
F32 = jnp.float32
BF16 = jnp.bfloat16


def call(body, outs, ins, in_specs=None, scratch=(), flops=0, out_specs=None):
    return pl.pallas_call(
        body,
        out_shape=outs,
        in_specs=in_specs or [VMEM] * len(ins),
        out_specs=out_specs or [VMEM] * len(outs),
        scratch_shapes=list(scratch),
        compiler_params=pltpu.CompilerParams(vmem_limit_bytes=LIMIT),
        cost_estimate=pl.CostEstimate(flops=flops, bytes_accessed=flops // 160, transcendentals=0),
    )(*ins)


def iota(shape, dim):
    return lax.broadcasted_iota(jnp.int32, shape, dim)


def dot(a, b, dims=((1,), (0,))):
    return lax.dot_general(a, b, (dims, ((), ())), preferred_element_type=F32)


def swaps(count):
    return count & (count - 1) == 0


def target(index, step, count):
    if swaps(count):
        return index ^ step if isinstance(index, int) else lax.bitwise_xor(index, step)
    return (index + step) % count if isinstance(index, int) else lax.rem(index + step, count)


def source(index, step, count):
    return target(index, step if swaps(count) else count - step, count)


def permute(value, axis, step, back=False):
    count = lax.axis_size(axis)
    pairs = [(i, target(i, step, count)) for i in range(count)]
    if back:
        pairs = [(j, i) for i, j in pairs]
    return lax.ppermute(value, axis, pairs)


def routing(ids, experts):
    choices, rows = ids.shape
    padded = -(-experts // ROWS) * ROWS
    expert_of = iota((padded, rows), 0)
    chosen = jnp.zeros((padded, rows), F32)
    for k in range(choices):
        chosen = chosen + jnp.where(ids[k : k + 1, :] == expert_of, 1.0, 0.0)
    before = jnp.where(iota((rows, rows), 0) < iota((rows, rows), 1), 1.0, 0.0)
    place = dot(chosen.astype(BF16), before.astype(BF16))
    return expert_of, chosen, place


def row_of(table, expert_of, expert):
    return jnp.sum(jnp.where(expert_of == expert, table, 0.0), axis=0, keepdims=True)


def selection(chosen, place, expert_of, expert, capacity):
    rows = chosen.shape[1]
    hit = row_of(chosen, expert_of, expert)
    at = row_of(place, expert_of, expert)
    return jnp.where((iota((capacity, rows), 0).astype(F32) == at) & (hit > 0.0), 1.0, 0.0)


class Piece:
    def __init__(self, step, lo, hi, cap, coded):
        self.step, self.lo, self.hi, self.cap, self.coded = step, lo, hi, cap, coded
        self.across = (hi - lo) // LANES
        self.length = cap * self.across + (ROWS if coded else 0)
        self.shape = jax.ShapeDtypeStruct((self.length, LANES), BF16)

    def covers(self, lo, hi):
        return self.lo <= lo and hi <= self.hi

    def place(self, r, c):
        start = (r * self.across + c) * ROWS
        return slice(start, start + ROWS)

    def store(self, ref, lo, value):
        first = (lo - self.lo) // LANES
        for r in range(self.cap // ROWS):
            for c in range(value.shape[1] // LANES):
                ref[self.place(r, first + c), :] = value[
                    r * ROWS : (r + 1) * ROWS, c * LANES : (c + 1) * LANES
                ]

    def load(self, ref, lo, hi):
        first, last = (lo - self.lo) // LANES, (hi - self.lo) // LANES
        rows = []
        for r in range(self.cap // ROWS):
            tiles = [ref[self.place(r, c), :] for c in range(first, last)]
            rows.append(jnp.concatenate(tiles, axis=1))
        return jnp.concatenate(rows, axis=0)

    def codes(self, ref):
        return ref[self.length - ROWS : self.length, :].astype(F32)[0:1, : self.cap]


def gather(pieces, refs, lo, hi):
    return jnp.concatenate(
        [p.load(r, lo, hi) for p, r in zip(pieces, refs) if p.covers(lo, hi)], axis=0
    )


def local(
    tokens,
    route_ids,
    route_weight,
    user_slot,
    gate_weight,
    up_weight,
    down_weight,
    adapter_down,
    adapter_up,
):
    experts = lax.axis_size("expert")
    hiddens = lax.axis_size("hidden")
    tok_rows, choices = route_ids.shape
    limit = tok_rows * choices * 3 // (2 * experts)
    cap = -(-limit // ROWS) * ROWS
    part = tokens.shape[1]
    half, quarter = part // 2, part // 4
    units = gate_weight.shape[2]
    adapt_cols = adapter_down.shape[2]
    slots = adapt_cols // RANK
    total = experts * cap
    users = user_slot.shape[0]
    steps = list(range(1, experts))
    last = experts - 1
    segments = [(0, half), (half, part)]

    there = []
    for k in range(experts):
        if k and k in (1, last):
            there += [Piece(k, 0, half, cap, True), Piece(k, half, part, cap, False)]
        else:
            there += [Piece(k, 0, part, cap, True)]
    home, first = [], experts // 2
    for k in range(experts):
        if k and k == first:
            home += [Piece(k, 0, half, cap, False), Piece(k, half, part, cap, False)]
        else:
            home += [Piece(k, 0, part, cap, False)]
    home_segments = [(0, quarter), (quarter, half), (half, part)]
    lead = max(0, min(i for i, p in enumerate(home) if p.step == first))

    def dispatch(ids_in, slot_in, tok_in, *refs):
        *outs, ids, slot, tok, sems = refs
        copies = [
            pltpu.make_async_copy(a, b, sems.at[i])
            for i, (a, b) in enumerate([(ids_in, ids), (slot_in, slot), (tok_in, tok)])
        ]
        for c in copies:
            c.start()
        me = lax.axis_index("expert")
        copies[0].wait()
        copies[1].wait()
        expert_of, chosen, place = routing(ids[...], experts)
        user_at = jnp.where(
            iota((users, tok_rows), 1) // USER_TOK == iota((users, tok_rows), 0), 1.0, 0.0
        )
        slots_of = dot(slot[...].astype(F32).astype(BF16), user_at.astype(BF16))
        picks, codes = [], []
        for k in range(experts):
            e = target(me, k, experts)
            pick = selection(chosen, place, expert_of, e, cap)
            pick = jnp.concatenate([pick, jnp.zeros((LANES - cap, tok_rows), F32)]).astype(BF16)
            own = row_of(slots_of, iota(slots_of.shape, 0), e)
            own = jnp.broadcast_to(own, (ROWS, tok_rows)).astype(BF16)
            codes.append(dot(own, pick, ((1,), (1,))).astype(BF16))
            picks.append(pick[:cap])
        copies[2].wait()
        rows = dot(jnp.concatenate(picks, axis=0), tok[...]).astype(BF16)
        for p, ref in zip(there, outs):
            p.store(ref, p.lo, rows[p.step * cap : (p.step + 1) * cap, p.lo : p.hi])
            if p.coded:
                ref[p.length - ROWS : p.length, :] = codes[p.step]

    sent = call(
        dispatch,
        [p.shape for p in there],
        tuple(pltpu.with_memory_space_constraint(v, pltpu.HBM) for v in (route_ids.T, user_slot.T, tokens)),
        in_specs=[HBM] * 3,
        scratch=[
            pltpu.VMEM(route_ids.T.shape, jnp.int32),
            pltpu.VMEM(user_slot.T.shape, jnp.int32),
            pltpu.VMEM(tokens.shape, BF16),
            pltpu.SemaphoreType.DMA((3,)),
        ],
    )

    def pace(inp, out):
        out[...] = inp[...]

    sent = [*call(pace, [there[0].shape], (sent[0],), flops=10**10), *sent[1:]]

    gate_w, up_w, down_w = (
        pltpu.with_memory_space_constraint(w[0], pltpu.VMEM)
        for w in (gate_weight, up_weight, down_weight)
    )

    arrived = [s if p.step == 0 else permute(s, "expert", p.step) for p, s in zip(there, sent)]
    others = [[permute(a, "hidden", d) for a in arrived] for d in range(1, hiddens)]

    def within(lo, hi, values):
        kept = [i for i, p in enumerate(there) if p.covers(lo, hi)]
        return [there[i] for i in kept], [values[i] for i in kept]

    def multiply(x, gate_ref, up_ref, start):
        at = pl.ds(pl.multiple_of(start, LANES), x.shape[1])
        return dot(x, gate_ref[at, :]), dot(x, up_ref[at, :])

    acc = [jax.ShapeDtypeStruct((total, units), F32)] * 2

    def row_codes(pieces, refs):
        return jnp.concatenate([p.codes(r) for p, r in zip(pieces, refs) if p.coded], axis=1)

    def slot_mask(codes):
        return (iota((adapt_cols, total), 0) // RANK).astype(F32) == codes

    ranks, pieces_a, values_a = None, *within(*segments[0], arrived)
    for s, (lo, hi) in enumerate(segments):
        pieces, values = within(lo, hi, arrived)

        def rank_step(*refs, lo=lo, hi=hi, s=s, pieces=pieces):
            x = gather(pieces, refs, lo, hi)
            full = dot(refs[len(pieces)][lo:hi, :], x, ((0,), (1,)))
            if s:
                full = full + refs[len(pieces) + 1][...]
                codes = row_codes(pieces_a, refs[len(pieces) + 2 :])
                full = jnp.where(slot_mask(codes), full, 0.0)
                full = jnp.sum(full.reshape(slots, RANK, total), axis=0)
            refs[-1][...] = full

        extra = () if ranks is None else (ranks, *values_a)
        shape = (adapt_cols if s == 0 else RANK, total)
        (ranks,) = call(
            rank_step, [jax.ShapeDtypeStruct(shape, F32)], (*values, adapter_down[0], *extra)
        )
    rank_others = [permute(ranks, "hidden", d) for d in range(1, hiddens)]

    sums = None
    for s, (lo, hi) in enumerate(segments):
        pieces, values = within(lo, hi, arrived)

        def own_step(*refs, lo=lo, hi=hi, s=s, pieces=pieces):
            n = len(pieces)
            gate, up = multiply(
                gather(pieces, refs, lo, hi),
                refs[n],
                refs[n + 1],
                lax.axis_index("hidden") * part + lo,
            )
            if s:
                gate, up = gate + refs[n + 2][...], up + refs[n + 3][...]
            refs[-2][...] = gate
            refs[-1][...] = up

        sums = call(own_step, acc, (*values, gate_w, up_w, *(sums or (down_w,))))

    def partner_parts(refs, lo, hi, gate_ref, up_ref, gate, up, pieces):
        for d in range(1, hiddens):
            base = source(lax.axis_index("hidden"), d, hiddens) * part + lo
            x = gather(pieces, refs[(d - 1) * len(pieces) : d * len(pieces)], lo, hi)
            g, u = multiply(x, gate_ref, up_ref, base)
            gate, up = gate + g, up + u
        return gate, up

    lo, hi = segments[0]
    pieces = within(lo, hi, there)[0]
    values = [v for o in others for v in within(lo, hi, o)[1]]

    def other_step(*refs):
        gate_ref, up_ref, gate_in, up_in, gate_out, up_out = refs[-6:]
        gate_out[...], up_out[...] = partner_parts(
            refs, *segments[0], gate_ref, up_ref, gate_in[...], up_in[...], pieces_a
        )

    sums = call(other_step, acc, (*values, gate_w, up_w, *sums))

    pieces_b = within(*segments[1], there)[0]
    values = [v for o in others for v in within(*segments[1], o)[1]]

    def store_down(act_rows, down_ref, base, lo, hi, pieces, refs, first):
        at = pl.ds(pl.multiple_of(base + lo, LANES), hi - lo)
        y = dot(act_rows, down_ref[:, at]).astype(BF16)
        for p, ref in zip(pieces, refs):
            if p.covers(lo, hi):
                n = p.step * cap - first
                p.store(ref, lo, y[n : n + cap])

    n_b = len(values)

    def activate(*refs):
        codes = row_codes(pieces_a, refs[n_b : n_b + len(pieces_a)])
        rest = refs[n_b + len(pieces_a) :]
        rank_refs, rest = rest[:hiddens], rest[hiddens:]
        gate_in, up_in, gate_ref, up_ref, factor, down_ref, act_ref = rest[:7]
        rank = rank_refs[0][...]
        for r in rank_refs[1:]:
            rank = rank + r[...]
        rank = jnp.broadcast_to(rank[None], (slots, RANK, total)).reshape(adapt_cols, total)
        rank = jnp.where(slot_mask(codes), rank, 0.0).astype(BF16)
        up = up_in[...] + dot(rank, factor[...], ((0,), (0,)))
        gate, up = partner_parts(
            refs, *segments[1], gate_ref, up_ref, gate_in[...], up, pieces_b
        )
        act = (gate / (1.0 + jnp.exp(-gate)) * up).astype(BF16)
        act_ref[...] = act
        p = home[lead]
        for d in range(1, hiddens):
            base = target(lax.axis_index("hidden"), d, hiddens) * part
            rows = act[p.step * cap : (p.step + 1) * cap]
            store_down(rows, down_ref, base, p.lo, p.hi, [p], [rest[6 + d]], p.step * cap)

    act, *lead_sent = call(
        activate,
        [jax.ShapeDtypeStruct((total, units), BF16)] + [home[lead].shape] * (hiddens - 1),
        (
            *values,
            *within(*segments[0], arrived)[1],
            ranks,
            *rank_others,
            *sums,
            gate_w,
            up_w,
            adapter_up[0],
            down_w,
        ),
    )

    def down(step, pieces, lead_too=False):
        def body(act_ref, down_ref, *outs):
            if lead_too:
                p = home[lead]
                rows = act_ref[p.step * cap : (p.step + 1) * cap, :]
                base = lax.axis_index("hidden") * part
                store_down(rows, down_ref, base, p.lo, p.hi, [p], outs[-1:], p.step * cap)
            base = target(lax.axis_index("hidden"), step, hiddens) * part if step else (
                lax.axis_index("hidden") * part
            )
            for lo, hi in home_segments:
                if any(p.covers(lo, hi) for p in pieces):
                    store_down(act_ref[...], down_ref, base, lo, hi, pieces, outs, 0)

        shapes = [p.shape for p in pieces] + [home[lead].shape] * lead_too
        return call(body, shapes, (act, down_w))

    rest = [i for i in range(len(home)) if i != lead]
    sent_home = []
    for d in range(1, hiddens):
        out = down(d, [home[i] for i in rest], d == 1)
        if d == 1:
            *out, lead_kept = out
        sent_home.append({lead: lead_sent[d - 1], **dict(zip(rest, out))})
    kept = {lead: lead_kept, **dict(zip(rest, down(0, [home[i] for i in rest])))}
    order = [lead] + ([lead + 1] if lead else [])
    order += [i for i in reversed(range(len(home))) if i not in order]
    summed = {
        i: [permute(sent_home[d - 1][i], "hidden", d) for d in range(1, hiddens)]
        for i in order
        if home[i].step > 1
    }

    def add(*refs):
        y = refs[0][...].astype(F32)
        for r in refs[1:-1]:
            y = y + r[...].astype(F32)
        refs[-1][...] = y.astype(BF16)

    returned = {}
    for i in order:
        if home[i].step > 1:
            (y,) = call(add, [home[i].shape], (kept[i], *summed[i]))
            returned[i] = permute(y, "expert", home[i].step, back=True)

    final = max([i for i in range(len(home)) if home[i].step not in (0, first)], default=0)
    early = [i for i in range(len(home)) if home[i].step > 1 and i != final]

    def mixing(ids, weight, chosen_steps):
        me = lax.axis_index("expert")
        expert_of, chosen, place = routing(ids, experts)
        weights_of = jnp.zeros(chosen.shape, F32)
        for j in range(choices):
            weights_of = weights_of + jnp.where(ids[j : j + 1] == expert_of, weight[j : j + 1], 0.0)
        mix = []
        for k in chosen_steps:
            e = target(me, k, experts)
            mix.append(
                selection(chosen, place, expert_of, e, cap) * row_of(weights_of, expert_of, e)
            )
        mix = jnp.concatenate(mix, axis=0)
        terms = []
        for _ in range(3):
            terms.append(mix.astype(BF16))
            mix = mix - terms[-1].astype(F32)
        return terms

    def mixed_sum(terms, rows):
        value = dot(jnp.concatenate(terms, axis=1), rows, ((0,), (0,)))
        return value[:tok_rows] + value[tok_rows : 2 * tok_rows] + value[2 * tok_rows :]

    early_steps = [k for k in steps if any(home[i].step == k for i in early)]
    tokens_tile = Piece(None, 0, part, tok_rows, False)

    near = [0, 1]
    near_parts = [[kept[i] for i in near]]
    near_parts += [[sent_home[d - 1][i] for i in near] for d in range(1, hiddens)]
    near_parts = [[own, permute(row, "expert", 1, back=True)] for own, row in near_parts]

    def near_mix(ids, weight, *refs):
        terms = mixing(ids[...], weight[...], near)
        for d in range(hiddens):
            own, row = refs[2 * d : 2 * d + 2]
            for lo, hi in segments:
                rows = jnp.concatenate(
                    [home[0].load(own, lo, hi), home[1].load(row, lo, hi)], axis=0
                )
                value = mixed_sum(terms, rows)
                if d:
                    tokens_tile.store(refs[2 * hiddens + d], lo, value.astype(BF16))
                else:
                    refs[2 * hiddens][:, lo:hi] = value

    near_kept, *near_away = call(
        near_mix,
        [jax.ShapeDtypeStruct((tok_rows, part), F32)] + [tokens_tile.shape] * (hiddens - 1),
        (route_ids.T, route_weight.T, *[v for pair in near_parts for v in pair]),
    )
    near_others = [permute(near_away[d - 1], "hidden", d) for d in range(1, hiddens)]

    def combine(*refs):
        terms = mixing(refs[0][...], refs[1][...], early_steps)
        for lo, hi in home_segments:
            rows = [home[i].load(r, lo, hi) for i, r in zip(early, refs[2:]) if home[i].covers(lo, hi)]
            refs[-4][:, lo:hi] = mixed_sum(terms, jnp.concatenate(rows, axis=0))
        for ref, t in zip(refs[-3:], mixing(refs[0][...], refs[1][...], [home[final].step])):
            ref[...] = t

    mixed, *final_terms = call(
        combine,
        [jax.ShapeDtypeStruct((tok_rows, part), F32)]
        + [jax.ShapeDtypeStruct((cap, tok_rows), BF16)] * 3,
        (route_ids.T, route_weight.T, *[returned[i] for i in early]),
    )

    def finish(partial, kept_sum, *refs):
        terms, refs = [r[...] for r in refs[:3]], refs[3:]
        row, others_in = refs[0], refs[1:hiddens]
        out, staged, sems = refs[-3:]
        copies = []
        for i, (lo, hi) in enumerate(home_segments):
            value = partial[:, lo:hi] + kept_sum[:, lo:hi]
            for r in others_in:
                value = value + tokens_tile.load(r, lo, hi).astype(F32)
            value = value + mixed_sum(terms, home[final].load(row, lo, hi))
            staged[:, lo:hi] = value.astype(BF16)
            copies.append(
                pltpu.make_async_copy(staged.at[:, lo:hi], out.at[:, lo:hi], sems.at[i])
            )
            copies[-1].start()
        for c in copies:
            c.wait()

    (result,) = call(
        finish,
        [jax.ShapeDtypeStruct((tok_rows, part), BF16)],
        (mixed, near_kept, *final_terms, returned[final], *near_others),
        out_specs=[ANY],
        scratch=[
            pltpu.VMEM((tok_rows, part), BF16),
            pltpu.SemaphoreType.DMA((len(home_segments),)),
        ],
    )
    return result


def solution(mesh):
    in_specs = (
        P(("parts", "expert", "rep"), "hidden"),
        P(("parts", "expert", "rep"), None),
        P(("parts", "expert", "rep"), None),
        P(("parts", "expert", "rep"), None),
        P("expert", None, "hidden"),
        P("expert", None, "hidden"),
        P("expert", "hidden", None),
        P("expert", "hidden", None),
        P("expert", None, "hidden"),
    )
    out_specs = P(("parts", "expert", "rep"), "hidden")

    return jax.shard_map(local, mesh=mesh, in_specs=in_specs, out_specs=out_specs, check_vma=False)
```
